32 devices in a mesh: band: 8 (over z, y), grid: 4 (over x, core).
Axes of the slice: x: 2, y: 2, z: 4, core: 2. Of those that a mesh axis runs over, the one named last changes fastest.
Arguments:
- orbitals: bfloat16 [16, 128, 128, 128], P('band', 'grid'), may hold values from -6 to 6
- occupation: float32 [16], replicated, may hold values from 0.25 to 2
- partner: int32 [8], replicated, may hold values from 0 to 7, as said below
- col_index: int32 [8192], replicated, may hold values from 0 to 16383, as said below
- kernel: float32 [128, 8192], P(None, 'grid'), may hold values from 0.1 to 4
Outputs:
- exchange: float32 [16, 128, 128, 128], P('band', 'grid')
The draws below stay inside these ranges and needn't reach their ends.
Inputs may be any that keep to these rules, and one draw needn't show every extreme that they name: partner[partner[a]] = a and partner[a] != a for every block a. `col_index`: all entries are distinct; the entries at positions g * 2048 to (g + 1) * 2048 - 1 are columns of the g-th block of 4096 consecutive columns, among them that block's first and last column.
All inputs are finite; a program needn't handle non-finite values.
Results may differ from the reference program's by a relative error of at most 0.0065.
Values may be sent and summed in bfloat16 or wider, within the bound.
No kernel may reach another device: no remote copies, remote signals or barrier semaphores. Data moves between devices by JAX's collectives and lax.ppermute only.
A program may use at most 64 MiB of HBM per device.

```python
import math
import jax
import jax.numpy as jnp
from jax import lax

NX = 128
NY = 128
NZ = 128
BLK = 2
BLOCKS = 8
BANDS = 16
PAIRS = 2
RANGE = 4096
COL_DEV = 2048
NCOL = 8192


def draw_partner(key, part):
    shuffled = jax.random.permutation(key, BLOCKS).astype(jnp.int32)
    flipped = shuffled.reshape(-1, 2)[:, ::-1].reshape(-1)
    return jnp.zeros((BLOCKS,), jnp.int32).at[shuffled].set(flipped)


def draw_col_index(key, part):
    group_count = NCOL // COL_DEV
    subkeys = jax.random.split(key, group_count)

    def pick_block(block_key, block_number):
        middle_cols = jax.random.permutation(jax.random.fold_in(block_key, 1), RANGE - 2)[:COL_DEV - 2].astype(jnp.int32) + 1
        ends_cols = jnp.array([0, RANGE - 1], jnp.int32)
        chosen = jnp.concatenate([ends_cols, middle_cols])
        chosen = jax.random.permutation(jax.random.fold_in(block_key, 2), chosen)
        return chosen + block_number * RANGE
    picked = jax.vmap(pick_block)(subkeys, jnp.arange(group_count, dtype=jnp.int32))
    return picked.reshape(-1).astype(jnp.int32)


def steps_of(key, extent, cuts, low, top_value):
    def one(position, parts):
        draws = jax.random.uniform(jax.random.fold_in(jax.random.fold_in(key, 6), position), (parts,), jnp.float32, low / len(cuts), top_value / len(cuts))
        return jnp.repeat(jnp.exp(draws), extent[position] // parts).reshape((-1,) + (1,) * (len(extent) - position - 1))

    gain = one(*cuts[0])
    for cut in cuts[1:]:
        gain = gain * one(*cut)
    return gain


def normal_values(key, dims, width, limit, cuts=(), kind=jnp.bfloat16):
    loudness = steps_of(key, dims, cuts, -0.22, 0.18) if cuts else 1.0
    drawn = jax.random.normal(key, dims, jnp.float32) * width * loudness
    return jnp.minimum(jnp.maximum(drawn, -limit), limit).astype(kind)


def setup_inputs(seed: int = 0) -> dict:
    streams_of = jax.random.split(jax.random.key(seed), 6)
    orbitals = normal_values(streams_of[0], (BANDS, NX, NY, NZ), 1.0, 6.0, ((0, 8), (1, 4)))
    occupation = jnp.clip(jnp.exp(jax.random.uniform(streams_of[1], (BANDS,), jnp.float32, math.log(0.25), math.log(2.0))), 0.25, 2.0)
    partner = draw_partner(jax.random.fold_in(streams_of[5], 71), 0)
    col_index = draw_col_index(jax.random.fold_in(streams_of[5], 71), 0)
    kernel = jnp.clip(jnp.exp(math.log(4.0) - 3.6888794 * jax.random.uniform(streams_of[4], (NX, NCOL), jnp.float32) ** steps_of(streams_of[4], (NX, NCOL), ((1, 4),), -0.2, 0.2)), 0.1, 4.0)
    return dict(orbitals=orbitals, occupation=occupation, partner=partner, col_index=col_index, kernel=kernel)


def tables(length):
    counter = jnp.arange(length, dtype=jnp.int32)
    product = (counter[:, None] * counter[None, :]) % length
    angles = product.astype(jnp.float32) * (2.0 * math.pi / length)
    return jnp.cos(angles).astype(jnp.bfloat16), jnp.sin(angles).astype(jnp.bfloat16)


def widen(values):
    return values.astype(jnp.float32)


def contract(pattern, left_side, right_side):
    return jnp.einsum(pattern, widen(left_side), widen(right_side), precision=lax.Precision.HIGHEST)


def pair_potentials(density, kern_full):
    xcosine, xsines = tables(NX)
    ycosine, ysines = tables(NY)
    zcosine, zsines = tables(NZ)
    pair_count = density.shape[0]
    first_real = contract('pxyz,zk->pxyk', density, zcosine).astype(jnp.bfloat16)
    first_imag = (-contract('pxyz,zk->pxyk', density, zsines)).astype(jnp.bfloat16)
    second_real = (contract('pxyk,yq->pxqk', first_real, ycosine) + contract('pxyk,yq->pxqk', first_imag, ysines)).astype(jnp.bfloat16)
    second_imag = (contract('pxyk,yq->pxqk', first_imag, ycosine) - contract('pxyk,yq->pxqk', first_real, ysines)).astype(jnp.bfloat16)
    second_real = second_real.reshape(pair_count, NX, NY * NZ)
    second_imag = second_imag.reshape(pair_count, NX, NY * NZ)
    scaled_real = contract('pxc,xk->pkc', second_real, xcosine) + contract('pxc,xk->pkc', second_imag, xsines)
    scaled_imag = contract('pxc,xk->pkc', second_imag, xcosine) - contract('pxc,xk->pkc', second_real, xsines)
    scaled_real = (scaled_real * kern_full).astype(jnp.bfloat16)
    scaled_imag = (scaled_imag * kern_full).astype(jnp.bfloat16)
    third_real = (contract('pkc,xk->pxc', scaled_real, xcosine) - contract('pkc,xk->pxc', scaled_imag, xsines)).astype(jnp.bfloat16)
    third_imag = (contract('pkc,xk->pxc', scaled_imag, xcosine) + contract('pkc,xk->pxc', scaled_real, xsines)).astype(jnp.bfloat16)
    third_real = third_real.reshape(pair_count, NX, NY, NZ)
    third_imag = third_imag.reshape(pair_count, NX, NY, NZ)
    fourth_real = (contract('pxqk,yq->pxyk', third_real, ycosine) - contract('pxqk,yq->pxyk', third_imag, ysines)).astype(jnp.bfloat16)
    fourth_imag = (contract('pxqk,yq->pxyk', third_imag, ycosine) + contract('pxqk,yq->pxyk', third_real, ysines)).astype(jnp.bfloat16)
    return contract('pxyk,zk->pxyz', fourth_real, zcosine) - contract('pxyk,zk->pxyz', fourth_imag, zsines)


def reference(orbitals, occupation, partner, col_index, kernel):
    norm_scale = 1.0 / (NX * NY * NZ)
    kern_full = jnp.zeros((NX, NY * NZ), jnp.float32).at[:, col_index].set(kernel * norm_scale)
    half_block = BLK // 2
    pair_slot = jnp.arange(PAIRS, dtype=jnp.int32)
    left_index = pair_slot // half_block
    band_slot = jnp.arange(BLK, dtype=jnp.int32)
    left_onehot = (left_index[None, :] == band_slot[:, None]).astype(jnp.float32)

    def visit_block(block_index, accumulated):
        block_index = jnp.asarray(block_index).astype(jnp.int32)
        partner_block = partner[block_index].astype(jnp.int32)
        parity = (block_index > partner_block).astype(jnp.int32)
        right_index = (left_index + parity) % 2 + 2 * (pair_slot % half_block)
        own_start = (block_index * BLK).astype(jnp.int32)
        their_start = (partner_block * BLK).astype(jnp.int32)
        own_bands = lax.dynamic_slice_in_dim(orbitals, own_start, BLK, 0)
        theirs = lax.dynamic_slice_in_dim(orbitals, their_start, BLK, 0)
        left_bands = jnp.take(own_bands, left_index, axis=0)
        right_bands = jnp.take(theirs, right_index, axis=0)
        density = (widen(left_bands) * widen(right_bands)).astype(jnp.bfloat16)
        potential = pair_potentials(density, kern_full)
        own_occ = lax.dynamic_slice_in_dim(occupation, own_start, BLK, 0)
        their_occ = lax.dynamic_slice_in_dim(occupation, their_start, BLK, 0)
        right_weight = jnp.take(their_occ, right_index)
        left_weight = jnp.take(own_occ, left_index)
        own_terms = (potential * right_weight[:, None, None, None]) * widen(right_bands)
        their_terms = (potential * left_weight[:, None, None, None]) * widen(left_bands)
        right_onehot = (right_index[None, :] == band_slot[:, None]).astype(jnp.float32)
        own_sum = jnp.einsum('np,pxyz->nxyz', left_onehot, own_terms, precision=lax.Precision.HIGHEST)
        their_sum = jnp.einsum('np,pxyz->nxyz', right_onehot, their_terms, precision=lax.Precision.HIGHEST)
        current = lax.dynamic_slice_in_dim(accumulated, own_start, BLK, 0)
        accumulated = lax.dynamic_update_slice_in_dim(accumulated, current + own_sum, own_start, 0)
        current = lax.dynamic_slice_in_dim(accumulated, their_start, BLK, 0)
        accumulated = lax.dynamic_update_slice_in_dim(accumulated, current + their_sum, their_start, 0)
        return accumulated

    accumulated = lax.fori_loop(0, BLOCKS, visit_block, jnp.zeros(orbitals.shape, jnp.float32))
    return -accumulated
```

```python
import functools
import math

import jax
import jax.numpy as jnp
from jax import lax
from jax.experimental import pallas as pl
from jax.experimental.pallas import tpu as pltpu
from jax.sharding import PartitionSpec as P


BF16 = jnp.bfloat16
F32 = jnp.float32


def tables(length):
    counter = jnp.arange(length, dtype=jnp.int32)
    product = counter[:, None] * counter[None, :] % length
    angles = product.astype(F32) * (2.0 * math.pi / length)
    return jnp.cos(angles).astype(BF16), jnp.sin(angles).astype(BF16)


def block_tables(length):
    cosine, sine = tables(length)
    left = jnp.concatenate(
        [jnp.concatenate([cosine, sine], 1), jnp.concatenate([-sine, cosine], 1)], 0
    )
    right = jnp.concatenate(
        [jnp.concatenate([cosine, -sine], 1), jnp.concatenate([sine, cosine], 1)], 0
    )
    return left, right


def dot(left_side, right_side):
    return jnp.dot(left_side, right_side, preferred_element_type=F32)


def cost(flops, moved):
    return pl.CostEstimate(flops=int(flops), bytes_accessed=int(moved), transcendentals=0)


def spec(shape, index=None):
    rank = len(shape)
    return pl.BlockSpec(shape, index or (lambda *_: (0,) * rank))


def expand_kernel(length, scale, own_ref, neg_ref, first_ref, cown_ref, cneg_ref, out_ref):
    rows, count = out_ref.shape[0], own_ref.shape[1]
    own = own_ref[...]
    high = own.astype(BF16)
    low = (own - high.astype(F32)).astype(BF16)
    both = jnp.concatenate([high, low], 0)
    neg = neg_ref[...]
    nx = own_ref.shape[0]
    wide = 2 * length
    lane = lax.broadcasted_iota(jnp.int32, (count, wide), 1)
    one = jnp.ones((count, wide), F32)
    zero = jnp.zeros((count, wide), F32)

    def step(pair, carry):
        target = lane + pair * wide
        pick = jnp.where(cown_ref[...] == target, one, zero).astype(BF16)
        mirror = jnp.where(cneg_ref[...] == target, one, zero).astype(BF16)
        found = dot(both, pick)
        total = found[:nx] + found[nx:] + dot(neg, mirror)
        for half in range(2):
            out_ref[2 * pair + half] = total[:, half * length : (half + 1) * length] * scale
        return carry

    lax.fori_loop(0, rows // 2, step, 0)
    out_ref[0] = out_ref[0] + first_ref[...] * scale


def expand(kernel, neg, first, cown, cneg, rows, length, scale):
    nx, count = kernel.shape
    return pl.pallas_call(
        functools.partial(expand_kernel, length, scale),
        out_shape=jax.ShapeDtypeStruct((rows, nx, length), F32),
        in_specs=[pl.BlockSpec(memory_space=pltpu.VMEM)] * 5,
        out_specs=pl.BlockSpec(memory_space=pltpu.VMEM),
        cost_estimate=cost(6 * nx * count * rows * length, 4 * nx * (count + rows * length)),
        name="expand",
    )(kernel, neg, first, cown, cneg)


def forward_kernel(own_ref, their_ref, zt_ref, yt_ref, *rest):
    out_refs, hold = rest[:-1], rest[-1]
    count, ny, nz = their_ref.shape
    zt, yt = zt_ref[...], yt_ref[...]

    def step(pair, carry):
        lines = []
        for k in range(2):
            x = 2 * pair + k
            theirs = their_ref[x]
            lines.append(jnp.concatenate([own_ref[0, x] * theirs, own_ref[1, x] * theirs], 1))
        first = dot(jnp.concatenate(lines, 0), zt).astype(BF16)
        stack = jnp.concatenate(
            [
                jnp.concatenate([first[:ny, :nz], first[ny:, :nz]], 1),
                jnp.concatenate([first[:ny, nz:], first[ny:, nz:]], 1),
            ],
            0,
        )
        second = dot(yt, stack)
        for k in range(2):
            for c in range(2):
                hold[c, pl.ds(2 * pair + k, ny, stride=count), :] = second[
                    c * ny : (c + 1) * ny, k * nz : (k + 1) * nz
                ]
        return carry

    lax.fori_loop(0, count // 2, step, 0, unroll=2)
    part = ny // len(out_refs)
    for slot, out_ref in enumerate(out_refs):
        for c in range(2):
            piece = hold[c, slot * part * count : (slot + 1) * part * count, :]
            out_ref[:, c] = piece.astype(BF16).reshape(part, count, nz)


def forward(own, their, part_number, zt, yt, groups):
    count, ny, nz = their.shape
    part = ny // groups
    shape = jax.ShapeDtypeStruct((part, 2, count, nz), BF16)
    return pl.pallas_call(
        forward_kernel,
        grid=(1,),
        out_shape=[shape] * groups,
        in_specs=[
            spec((2, count, ny, nz), lambda i: (0, part_number, 0, 0)),
            spec(their.shape),
            spec(zt.shape),
            spec(yt.shape),
        ],
        out_specs=[spec(shape.shape)] * groups,
        scratch_shapes=[pltpu.VMEM((2, ny * count, nz), F32)],
        cost_estimate=cost(2 * count * ny * nz * 2 * (2 * ny + 2 * nz), 10 * count * ny * nz),
        name="forward",
    )(own, their, zt, yt)


def middle_kernel(groups, halves, *refs):
    in_refs = refs[: groups * halves]
    kern_ref, xt_ref, ixt_ref = refs[groups * halves : groups * halves + 3]
    out_refs, hold = refs[groups * halves + 3 : -1], refs[-1]
    count, nx, nz = kern_ref.shape
    xt, ixt = xt_ref[...], ixt_ref[...]

    def step(pair, carry):
        lines, factors = [], []
        for k in range(2):
            line = 2 * pair + k
            lines.append(jnp.concatenate([r[line, c] for c in range(2) for r in in_refs], 0))
            factors.append(kern_ref[line])
        factor = jnp.concatenate(factors, 1)
        spectrum = dot(xt, jnp.concatenate(lines, 1))
        scaled = jnp.concatenate(
            [(spectrum[:nx] * factor).astype(BF16), (spectrum[nx:] * factor).astype(BF16)], 0
        )
        third = dot(ixt, scaled)
        for k in range(2):
            for c in range(2):
                hold[c, pl.ds(2 * pair + k, nx, stride=count), :] = third[
                    c * nx : (c + 1) * nx, k * nz : (k + 1) * nz
                ]
        return carry

    lax.fori_loop(0, count // 2, step, 0, unroll=2)
    rows = nx // (groups * halves)
    for number, out_ref in enumerate(out_refs):
        for c in range(2):
            piece = hold[c, number * rows * count : (number + 1) * rows * count, :]
            out_ref[:, c] = piece.astype(BF16).reshape(rows, count, nz)


def middle(pieces, kern, xt, ixt, groups, halves):
    count, nx, nz = kern.shape
    rows = nx // (groups * halves)
    shape = jax.ShapeDtypeStruct((rows, 2, count, nz), BF16)
    vmem = pl.BlockSpec(memory_space=pltpu.VMEM)
    return pl.pallas_call(
        functools.partial(middle_kernel, groups, halves),
        out_shape=[shape] * (groups * halves),
        in_specs=[vmem] * (groups * halves + 3),
        out_specs=[vmem] * (groups * halves),
        scratch_shapes=[pltpu.VMEM((2, nx * count, nz), F32)],
        cost_estimate=cost(16 * nx * nx * count * nz, 12 * count * nx * nz),
        name="middle",
    )(*pieces, kern, xt, ixt)


def backward_kernel(groups, has_total, *refs):
    in_refs = refs[:groups]
    their_ref, weight_ref, yt_ref, zt_ref = refs[groups : groups + 4]
    total_ref = refs[groups + 4] if has_total == 2 else None
    out_ref = refs[-1]
    count, ny, nz = their_ref.shape
    zt, yt = zt_ref[...], yt_ref[...]
    weight = weight_ref[0]

    def step(pair, carry):
        lines = []
        for k in range(2):
            x = 2 * pair + k
            lines.append(jnp.concatenate([r[x, c] for c in range(2) for r in in_refs], 0))
        fourth = dot(yt, jnp.concatenate(lines, 1)).astype(BF16)
        stack = jnp.concatenate(
            [
                jnp.concatenate([fourth[:ny, k * nz : (k + 1) * nz], fourth[ny:, k * nz : (k + 1) * nz]], 1)
                for k in range(2)
            ],
            0,
        )
        potential = dot(stack, zt)
        for k in range(2):
            x = 2 * pair + k
            theirs = their_ref[x].astype(F32) * weight
            for n in range(2):
                term = potential[k * ny : (k + 1) * ny, n * nz : (n + 1) * nz] * theirs
                if total_ref is None:
                    out_ref[n, x] = -term
                else:
                    out_ref[n, x] = total_ref[n, x] - term
        return carry

    lax.fori_loop(0, count // 2, step, 0, unroll=2)


def backward(pieces, their, weight, yt, zt, total, accumulate, part_number, slab):
    groups = len(pieces)
    count, ny, nz = their.shape
    vmem = pl.BlockSpec(memory_space=pltpu.VMEM)
    block = spec((2, count, ny, nz), lambda i: (0, part_number, 0, 0))
    has_total = 0 if total is None else (2 if accumulate else 1)
    extra = [] if total is None else [total]
    extra_specs = [] if total is None else [block if accumulate else pl.BlockSpec(memory_space=pl.ANY)]
    return pl.pallas_call(
        functools.partial(backward_kernel, groups, has_total),
        grid=(1,),
        out_shape=jax.ShapeDtypeStruct((2, slab, ny, nz), F32),
        in_specs=[spec(p.shape) for p in pieces]
        + [spec(their.shape), pl.BlockSpec(memory_space=pltpu.SMEM), spec(yt.shape), spec(zt.shape)]
        + extra_specs,
        out_specs=block,
        input_output_aliases={groups + 4: 0} if extra else {},
        cost_estimate=cost(2 * count * ny * nz * 2 * (2 * ny + 2 * nz), 24 * count * ny * nz),
        name="backward",
    )(*pieces, their, weight, yt, zt, *extra)


SPLIT = (1, 2)


def fetch(value, partner, after):
    if after is not None:
        value, _ = lax.optimization_barrier((value, after))
    size = lax.axis_size("band")
    rows, ny, nz = value.shape
    tile = 16
    spread = lax.all_to_all(
        value.reshape(rows * ny // tile, tile, nz), "band", split_axis=0, concat_axis=0, tiled=True
    )
    pieces = spread.reshape(size, rows * ny // (tile * size), tile, nz)
    chosen = jnp.take(pieces, partner, axis=0).reshape(spread.shape)
    return lax.all_to_all(chosen, "band", split_axis=0, concat_axis=0, tiled=True).reshape(value.shape)


def shift(value, axis, size, mask):
    return lax.ppermute(value, axis, [(i, i ^ mask) for i in range(size)])


def local(orbitals, occupation, partner, col_index, kernel):
    band_count, groups = lax.axis_size("band"), lax.axis_size("grid")
    slab, ny, nz = orbitals.shape[1:]
    nx, column_count = kernel.shape
    lines = ny // groups
    band_pos, me = lax.axis_index("band"), lax.axis_index("grid")

    theirs, starts, last = [], [], None
    for m in range(2):
        count = SPLIT[m] if slab % (16 * SPLIT[m]) == 0 else 1
        rows = slab // count
        starts.append(count)
        theirs.append([])
        for h in range(count):
            piece = lax.slice(orbitals, (m, h * rows, 0, 0), (m + 1, (h + 1) * rows, ny, nz))
            last = fetch(piece.reshape(rows, ny, nz), partner, last)
            theirs[m].append(last)

    span = lines * nz
    mirrored = jnp.roll(kernel[::-1], 1, axis=0).astype(BF16)
    mirror_of = [(i, groups - 1 - i) for i in range(groups)]
    mirror_first = [(i, (groups - i) % groups) for i in range(groups)]
    neg = lax.ppermute(mirrored, "grid", mirror_of)

    def columns(owner):
        return lax.dynamic_slice_in_dim(col_index, owner * column_count, column_count, 0)

    def flipped(cols):
        return (ny - cols // nz) % ny * nz + (nz - cols % nz) % nz

    mine = columns(me)
    cown = mine - me * span
    cneg = flipped(columns(groups - 1 - me)) - me * span
    kz_first = jnp.where(cown < nz, (nz - cown) % nz, -1)
    one_hot = (kz_first[:, None] == jnp.arange(nz, dtype=jnp.int32)[None, :]).astype(BF16)
    first = lax.ppermute(dot(mirrored, one_hot).astype(BF16), "grid", mirror_first).astype(F32)
    kern = expand(
        kernel, neg, first, cown[:, None], cneg[:, None], lines, nz, 0.5 / (nx * ny * nz)
    )

    def slots(table, axis):
        blocks = table.reshape(table.shape[:axis] + (2, groups, table.shape[axis] // (2 * groups)) + table.shape[axis + 1 :])
        order = jnp.arange(groups, dtype=jnp.int32) ^ me
        return jnp.take(blocks, order, axis=axis + 1).reshape(table.shape)

    xleft, xright = block_tables(nx)
    yleft, yright = block_tables(ny)
    zleft, zright = block_tables(nz)
    y_forward, x_forward = slots(yleft, 0), slots(xleft, 1)
    x_inverse, y_inverse = slots(xright, 0), slots(yright, 1)

    def swap(value, slot):
        return shift(value, "grid", groups, slot) if slot else value

    partner_block = partner[band_pos]
    total = None
    spectra = []
    for m in range(2):
        pieces = [[None] * starts[m] for _ in range(groups)]
        for h in range(starts[m]):
            sent = forward(orbitals, theirs[m][h], h, zright, y_forward, groups)
            for slot in range(groups):
                pieces[slot][h] = swap(sent[slot], slot)
        spectra.append(pieces)
    for m in range(2):
        flat = [piece for per_slot in spectra[m] for piece in per_slot]
        halves = starts[m]
        answers = middle(flat, kern, x_forward, x_inverse, groups, halves)
        weight = lax.dynamic_slice_in_dim(occupation, partner_block * 2 + m, 1, 0)
        for h in range(halves):
            arrived = [swap(answers[slot * halves + h], slot) for slot in range(groups)]
            total = backward(
                arrived, theirs[m][h], weight, y_inverse, zleft, total, m > 0, h, slab
            )
    return total


def solution(mesh):
    in_specs = (P("band", "grid", None, None), P(), P(), P(), P(None, "grid"))
    out_specs = P("band", "grid", None, None)
    return jax.shard_map(local, mesh=mesh, in_specs=in_specs, out_specs=out_specs, check_vma=False)
```

```python
import functools
import math

import jax
import jax.numpy as jnp
from jax import lax
from jax.experimental import pallas as pl
from jax.experimental.pallas import tpu as pltpu
from jax.sharding import PartitionSpec as P


BF16 = jnp.bfloat16
F32 = jnp.float32


def tables(length):
    counter = jnp.arange(length, dtype=jnp.int32)
    product = counter[:, None] * counter[None, :] % length
    angles = product.astype(F32) * (2.0 * math.pi / length)
    return jnp.cos(angles).astype(BF16), jnp.sin(angles).astype(BF16)


def block_tables(length):
    cosine, sine = tables(length)
    left = jnp.concatenate(
        [jnp.concatenate([cosine, sine], 1), jnp.concatenate([-sine, cosine], 1)], 0
    )
    right = jnp.concatenate(
        [jnp.concatenate([cosine, -sine], 1), jnp.concatenate([sine, cosine], 1)], 0
    )
    return left, right


def dot(left_side, right_side):
    return jnp.dot(left_side, right_side, preferred_element_type=F32)


def cost(flops, moved):
    return pl.CostEstimate(flops=int(flops), bytes_accessed=int(moved), transcendentals=0)


def spec(shape, index=None):
    rank = len(shape)
    return pl.BlockSpec(shape, index or (lambda *_: (0,) * rank))


SCALARS = pl.BlockSpec(memory_space=pltpu.SMEM)
WHOLE = pl.BlockSpec(memory_space=pltpu.VMEM)
UNROLL = 8
LANES = 128


def column_row(cols_ref, owner, count):
    return cols_ref[:, pl.ds(pl.multiple_of(owner * count, LANES), count)]


def flip(cols, ny, nz):
    return lax.rem(ny - cols // nz, ny) * nz + lax.rem(nz - cols % nz, nz)


def one_hot(row, base, size):
    position = lax.broadcasted_iota(jnp.int32, (size, row.shape[1]), 0) + base
    return jnp.where(row == position, 1.0, 0.0).astype(BF16)


def dot_t(left_side, right_side):
    dims = (((1,), (1,)), ((), ()))
    return lax.dot_general(left_side, right_side, dims, preferred_element_type=F32)


def mirror_kernel(span, nz, me_ref, kernel_ref, cols_ref, out_ref, first_ref):
    nx, count = kernel_ref.shape
    row = lax.broadcasted_iota(jnp.int32, (nx, nx), 0)
    column = lax.broadcasted_iota(jnp.int32, (nx, nx), 1)
    swap = jnp.where(lax.rem(row + column, nx) == 0, 1.0, 0.0).astype(BF16)
    mirrored = dot(swap, kernel_ref[...].astype(BF16)).astype(BF16)
    out_ref[...] = mirrored
    local_cols = column_row(cols_ref, me_ref[0], count) - me_ref[0] * span
    target = jnp.where(local_cols < nz, lax.rem(nz - local_cols, nz), -1)
    first_ref[...] = dot_t(mirrored, one_hot(target, 0, nz)).astype(BF16)


def mirror(me, kernel, cols, span, nz):
    nx = kernel.shape[0]
    return pl.pallas_call(
        functools.partial(mirror_kernel, span, nz),
        out_shape=[jax.ShapeDtypeStruct(kernel.shape, BF16), jax.ShapeDtypeStruct((nx, nz), BF16)],
        in_specs=[SCALARS, WHOLE, WHOLE],
        out_specs=[WHOLE] * 2,
        cost_estimate=cost(2 * nx * nx * kernel.shape[1], 6 * kernel.size),
        name="mirror",
    )(me, kernel, cols)


def expand_kernel(scale, groups, span, ny, me_ref, own_ref, neg_ref, first_ref, cols_ref, out_ref, hot):
    nx, count = own_ref.shape
    length = out_ref.shape[2]
    wide = 2 * length
    me = me_ref[0]
    both = jnp.concatenate([own_ref[...].astype(BF16), neg_ref[...]], 1)
    mine = column_row(cols_ref, me, count) - me * span
    theirs = flip(column_row(cols_ref, groups - 1 - me, count), ny, length) - me * span
    group = jnp.concatenate([mine, theirs + span], 1) // wide
    group = group - jnp.concatenate(
        [jnp.zeros((1, count), jnp.int32), jnp.full((1, count), span // wide, jnp.int32)], 1
    )
    hot[:, :count] = one_hot(mine & (wide - 1), 0, wide)
    hot[:, count:] = one_hot(theirs & (wide - 1), 0, wide)

    def step(number, carry):
        sides = []
        for k in range(2):
            wanted = jnp.where(group == 2 * number + k, 1.0, 0.0).astype(BF16)
            sides.append(both * wanted)
        total = dot_t(jnp.concatenate(sides, 0), hot[...])
        for k in range(2):
            for half in range(2):
                out_ref[4 * number + 2 * k + half] = (
                    total[k * nx : (k + 1) * nx, half * length : (half + 1) * length] * scale
                )
        return carry

    lax.fori_loop(0, out_ref.shape[0] // 4, step, 0)
    out_ref[0] = out_ref[0] + first_ref[...].astype(F32) * scale


def expand(me, kernel, neg, first, cols, groups, ny, length, scale):
    nx, count = kernel.shape
    rows = ny // groups
    return pl.pallas_call(
        functools.partial(expand_kernel, scale, groups, rows * length, ny),
        out_shape=jax.ShapeDtypeStruct((rows, nx, length), F32),
        in_specs=[SCALARS] + [WHOLE] * 4,
        out_specs=WHOLE,
        scratch_shapes=[pltpu.VMEM((2 * length, 2 * count), BF16)],
        cost_estimate=cost(4 * nx * count * rows * length, 4 * nx * (count + rows * length)),
        name="expand",
    )(me, kernel, neg, first, cols)


def forward_kernel(parts, base, me_ref, grid_ref, own_ref, *refs):
    piece_refs = refs[:parts]
    if parts > 1:
        zt_ref, yt_ref, their_ref = refs[parts : parts + 3]
        per = piece_refs[0].shape[0]
        for slot, piece_ref in enumerate(piece_refs):
            their_ref[pl.ds((me_ref[0] ^ slot) * per, per)] = piece_ref[...]
    else:
        their_ref, zt_ref, yt_ref = refs[:3]
    out_refs, hold = refs[3 + parts - (parts == 1) : -1], refs[-1]
    count, ny, nz = own_ref.shape[1:]
    tiles = ny // their_ref.shape[1]
    zt, yt = zt_ref[...], yt_ref[...]

    def step(pair, carry):
        lines = []
        for k in range(2):
            x = 2 * pair + k
            theirs = their_ref[pl.ds((base + x) * tiles, tiles)].reshape(ny, nz)
            lines.append(jnp.concatenate([own_ref[0, x] * theirs, own_ref[1, x] * theirs], 1))
        first = dot(jnp.concatenate(lines, 0), zt).astype(BF16)
        stack = jnp.concatenate(
            [
                jnp.concatenate([first[:ny, :nz], first[ny:, :nz]], 1),
                jnp.concatenate([first[:ny, nz:], first[ny:, nz:]], 1),
            ],
            0,
        )
        second = dot(yt, stack)
        for k in range(2):
            for c in range(2):
                hold[c, pl.ds(2 * pair + k, ny, stride=count), :] = second[
                    c * ny : (c + 1) * ny, k * nz : (k + 1) * nz
                ]
        return carry

    lax.fori_loop(0, count // 2, step, 0, unroll=min(UNROLL, count // 2))
    part = ny // len(out_refs)
    for slot, out_ref in enumerate(out_refs):
        begin = (grid_ref[0] ^ slot) * (part * count)
        for c in range(2):
            piece = hold[c, pl.ds(begin, part * count), :]
            out_ref[:, c] = piece.astype(BF16).reshape(part, count, nz)


def forward(me, grid_pos, own, pieces, half, count, zt, yt, groups):
    ny, nz = own.shape[2:]
    part = ny // groups
    parts = len(pieces)
    shape = jax.ShapeDtypeStruct((part, 2, count, nz), BF16)
    their = jax.ShapeDtypeStruct((parts * pieces[0].shape[0],) + pieces[0].shape[1:], BF16)
    outs = ([their] if parts > 1 else []) + [shape] * groups
    return pl.pallas_call(
        functools.partial(forward_kernel, parts, half * count),
        grid=(1,),
        out_shape=outs,
        in_specs=[SCALARS, SCALARS, spec((2, count, ny, nz), lambda i: (0, half, 0, 0))]
        + [spec(p.shape) for p in pieces]
        + [spec(zt.shape), spec(yt.shape)],
        out_specs=[spec(o.shape) for o in outs],
        scratch_shapes=[pltpu.VMEM((2, ny * count, nz), F32)],
        cost_estimate=cost(2 * count * ny * nz * 2 * (2 * ny + 2 * nz), 12 * count * ny * nz),
        name="forward",
    )(me, grid_pos, own, *pieces, zt, yt)


def middle_kernel(groups, halves, grid_ref, *refs):
    in_refs = refs[: groups * halves]
    kern_ref, xt_ref, ixt_ref = refs[groups * halves : groups * halves + 3]
    out_refs, hold = refs[groups * halves + 3 : -1], refs[-1]
    count, nx, nz = kern_ref.shape
    xt, ixt = xt_ref[...], ixt_ref[...]

    def step(pair, carry):
        lines, factors = [], []
        for k in range(2):
            line = 2 * pair + k
            lines.append(jnp.concatenate([r[line, c] for c in range(2) for r in in_refs], 0))
            factors.append(kern_ref[line])
        factor = jnp.concatenate(factors, 1)
        spectrum = dot(xt, jnp.concatenate(lines, 1))
        scaled = jnp.concatenate(
            [(spectrum[:nx] * factor).astype(BF16), (spectrum[nx:] * factor).astype(BF16)], 0
        )
        third = dot(ixt, scaled)
        for k in range(2):
            for c in range(2):
                hold[c, pl.ds(2 * pair + k, nx, stride=count), :] = third[
                    c * nx : (c + 1) * nx, k * nz : (k + 1) * nz
                ]
        return carry

    lax.fori_loop(0, count // 2, step, 0, unroll=min(UNROLL, count // 2))
    rows = nx // (groups * halves)
    for number, out_ref in enumerate(out_refs):
        owner = grid_ref[0] ^ (number // halves)
        begin = (owner * halves + number % halves) * (rows * count)
        for c in range(2):
            piece = hold[c, pl.ds(begin, rows * count), :]
            out_ref[:, c] = piece.astype(BF16).reshape(rows, count, nz)


def middle(grid_pos, pieces, kern, xt, ixt, groups, halves):
    count, nx, nz = kern.shape
    rows = nx // (groups * halves)
    shape = jax.ShapeDtypeStruct((rows, 2, count, nz), BF16)
    vmem = pl.BlockSpec(memory_space=pltpu.VMEM)
    return pl.pallas_call(
        functools.partial(middle_kernel, groups, halves),
        out_shape=[shape] * (groups * halves),
        in_specs=[SCALARS] + [vmem] * (groups * halves + 3),
        out_specs=[vmem] * (groups * halves),
        scratch_shapes=[pltpu.VMEM((2, nx * count, nz), F32)],
        cost_estimate=cost(16 * nx * nx * count * nz, 12 * count * nx * nz),
        name="middle",
    )(grid_pos, *pieces, kern, xt, ixt)


def backward_kernel(groups, has_total, base, *refs):
    in_refs = refs[:groups]
    their_ref, weight_ref, yt_ref, zt_ref = refs[groups : groups + 4]
    total_ref = refs[groups + 4] if has_total == 2 else None
    out_ref = refs[-1]
    count, ny, nz = out_ref.shape[1:]
    tiles = ny // their_ref.shape[1]
    zt, yt = zt_ref[...], yt_ref[...]
    weight = weight_ref[0]

    def step(pair, carry):
        lines = []
        for k in range(2):
            x = 2 * pair + k
            lines.append(jnp.concatenate([r[x, c] for c in range(2) for r in in_refs], 0))
        fourth = dot(yt, jnp.concatenate(lines, 1)).astype(BF16)
        stack = jnp.concatenate(
            [
                jnp.concatenate([fourth[:ny, k * nz : (k + 1) * nz], fourth[ny:, k * nz : (k + 1) * nz]], 1)
                for k in range(2)
            ],
            0,
        )
        potential = dot(stack, zt)
        for k in range(2):
            x = 2 * pair + k
            theirs = their_ref[pl.ds((base + x) * tiles, tiles)].reshape(ny, nz).astype(F32) * weight
            for n in range(2):
                term = potential[k * ny : (k + 1) * ny, n * nz : (n + 1) * nz] * theirs
                if total_ref is None:
                    out_ref[n, x] = -term
                else:
                    out_ref[n, x] = total_ref[n, x] - term
        return carry

    lax.fori_loop(0, count // 2, step, 0, unroll=min(UNROLL, count // 2))


def backward(pieces, their, weight, yt, zt, total, accumulate, part_number, slab):
    groups = len(pieces)
    count, ny, nz = pieces[0].shape[0], pieces[0].shape[2] * groups, pieces[0].shape[3]
    block = spec((2, count, ny, nz), lambda i: (0, part_number, 0, 0))
    has_total = 0 if total is None else (2 if accumulate else 1)
    extra = [] if total is None else [total]
    extra_specs = [] if total is None else [block if accumulate else pl.BlockSpec(memory_space=pl.ANY)]
    return pl.pallas_call(
        functools.partial(backward_kernel, groups, has_total, part_number * count),
        grid=(1,),
        out_shape=jax.ShapeDtypeStruct((2, slab, ny, nz), F32),
        in_specs=[spec(p.shape) for p in pieces]
        + [spec(their.shape), pl.BlockSpec(memory_space=pltpu.SMEM), spec(yt.shape), spec(zt.shape)]
        + extra_specs,
        out_specs=block,
        input_output_aliases={groups + 4: 0} if extra else {},
        cost_estimate=cost(2 * count * ny * nz * 2 * (2 * ny + 2 * nz), 24 * count * ny * nz),
        name="backward",
    )(*pieces, their, weight, yt, zt, *extra)


HALVES = (1, 2)
TILE = 16


def after(value, *others):
    return lax.optimization_barrier((value, others))[0]


def shift(value, axis, size, mask):
    return lax.ppermute(value, axis, [(i, i ^ mask) for i in range(size)]) if mask else value


def split_kernel(me_ref, in_ref, *out_refs):
    per = out_refs[0].shape[0]
    for slot, out_ref in enumerate(out_refs):
        out_ref[...] = in_ref[0, pl.ds((me_ref[0] ^ slot) * per, per)]


def split(me, value, band, chunk, tiles, parts):
    shape = jax.ShapeDtypeStruct((tiles // parts,) + value.shape[2:], value.dtype)
    return pl.pallas_call(
        split_kernel,
        grid=(1,),
        out_shape=[shape] * parts,
        in_specs=[SCALARS, spec((1, tiles) + value.shape[2:], lambda i: (band, chunk, 0, 0))],
        out_specs=[spec(shape.shape)] * parts,
        cost_estimate=cost(0, 4 * tiles * TILE * value.shape[3]),
        name="split",
    )(me, value)


def pick_kernel(parts, choice_ref, *refs):
    in_refs, out_refs, hold = refs[:parts], refs[parts:-1], refs[-1]
    for slot, in_ref in enumerate(in_refs):
        hold[slot] = in_ref[...]
    for slot, out_ref in enumerate(out_refs):
        out_ref[...] = hold[choice_ref[slot]]


def pick(choice, pieces):
    parts, shape = len(pieces), pieces[0].shape
    return pl.pallas_call(
        functools.partial(pick_kernel, parts),
        out_shape=[jax.ShapeDtypeStruct(shape, pieces[0].dtype)] * parts,
        in_specs=[SCALARS] + [WHOLE] * parts,
        out_specs=[WHOLE] * parts,
        scratch_shapes=[pltpu.VMEM((parts,) + shape, pieces[0].dtype)],
        cost_estimate=cost(0, 4 * parts * math.prod(shape)),
        name="pick",
    )(choice, *pieces)


def pick_stacked_kernel(parts, choice_ref, *refs):
    in_refs, out_ref, hold = refs[:parts], refs[-2], refs[-1]
    for slot, in_ref in enumerate(in_refs):
        hold[slot] = in_ref[...]
    for number in range(parts):
        out_ref[number] = hold[choice_ref[number]]


def pick_stacked(choice, pieces):
    parts, shape = len(pieces), pieces[0].shape
    return pl.pallas_call(
        functools.partial(pick_stacked_kernel, parts),
        out_shape=jax.ShapeDtypeStruct((parts,) + shape, pieces[0].dtype),
        in_specs=[SCALARS] + [WHOLE] * parts,
        out_specs=WHOLE,
        scratch_shapes=[pltpu.VMEM((parts,) + shape, pieces[0].dtype)],
        cost_estimate=cost(0, 4 * parts * math.prod(shape)),
        name="pick",
    )(choice, *pieces)


def local(orbitals, occupation, partner, col_index, kernel):
    bands, groups = lax.axis_size("band"), lax.axis_size("grid")
    slab, ny, nz = orbitals.shape[1:]
    nx, _ = kernel.shape
    lines = ny // groups
    band_pos, me = lax.axis_index("band"), lax.axis_index("grid")
    band_slots = jnp.arange(bands, dtype=jnp.int32)
    my_band = band_pos.astype(jnp.int32).reshape(1)
    choice = jnp.take(partner, band_slots ^ band_pos) ^ band_pos
    pick_choice = partner ^ band_pos
    tiled = orbitals.reshape(2, slab * ny // TILE, TILE, nz)

    def swap(value, slot):
        return shift(value, "grid", groups, slot)

    def exchange(value):
        return lax.all_to_all(value, "band", split_axis=0, concat_axis=0, tiled=True)

    def slotwise(sent):
        return [shift(piece, "band", bands, slot) for slot, piece in enumerate(sent)]

    my_grid = me.astype(jnp.int32).reshape(1)
    cols = col_index.reshape(1, -1)
    sent = split(my_band, tiled, 0, 0, slab * ny // TILE, bands)
    arrived = slotwise(sent)
    sent1 = split(my_band, after(tiled, *sent), 1, 0, slab * ny // TILE, bands)

    mirror_of = [(i, groups - 1 - i) for i in range(groups)]
    mirror_first = [(i, (groups - i) % groups) for i in range(groups)]
    mirrored, first_line = mirror(my_grid, after(kernel, *sent), cols, lines * nz, nz)
    neg = lax.ppermute(mirrored, "grid", mirror_of)
    first = lax.ppermute(first_line, "grid", mirror_first)

    def slots(table, axis):
        shape = table.shape
        blocks = table.reshape(shape[:axis] + (2, groups, shape[axis] // (2 * groups)) + shape[axis + 1 :])
        order = jnp.arange(groups, dtype=jnp.int32) ^ me
        return jnp.take(blocks, order, axis=axis + 1).reshape(shape)

    xleft, xright = block_tables(nx)
    yleft, yright = block_tables(ny)
    zleft, zright = block_tables(nz)
    x_forward, y_inverse = slots(xleft, 1), slots(yright, 1)
    theirs, answers, counts = [], [], []
    for m in range(2):
        halves = HALVES[m] if slab % (16 * HALVES[m]) == 0 else 1
        rows = slab // halves
        if m == 0:
            picked = pick(choice, after(arrived, mirrored, first_line, *sent1))
            fetched = slotwise(picked)
            kern = expand(
                my_grid, after(kernel, *picked), neg, first, cols, groups, ny, nz, 0.5 / (nx * ny * nz)
            )
            arrived = slotwise(after(sent1, *picked))
            their, *sent = forward(my_band, my_grid, orbitals, fetched, 0, rows, zright, yleft, groups)
        else:
            picked = pick_stacked(pick_choice, after(arrived, *sent))
            their = exchange(picked.reshape(tiled.shape[1:]))
            their = after(their, *answers[0])
            sent = forward(my_band, my_grid, orbitals, [their], 0, rows, zright, yleft, groups)
        pieces = [[swap(value, slot)] for slot, value in enumerate(sent)]
        for h in range(1, halves):
            more = forward(my_band, my_grid, orbitals, [their], h, rows, zright, yleft, groups)
            for slot, value in enumerate(more):
                pieces[slot].append(swap(value, slot))
        flat = [piece for per_slot in pieces for piece in per_slot]
        answers.append(middle(my_grid, flat, kern, x_forward, xright, groups, halves))
        theirs.append(their)
        counts.append(halves)

    total = None
    for m in range(2):
        weight = lax.dynamic_slice_in_dim(occupation, partner[band_pos] * 2 + m, 1, 0)
        for h in range(counts[m]):
            back = [swap(answers[m][slot * counts[m] + h], slot) for slot in range(groups)]
            if m == 0:
                back = after(back, *answers[1])
            total = backward(back, theirs[m], weight, y_inverse, zleft, total, m > 0, h, slab)
    return total


def solution(mesh):
    in_specs = (P("band", "grid", None, None), P(), P(), P(), P(None, "grid"))
    out_specs = P("band", "grid", None, None)
    return jax.shard_map(local, mesh=mesh, in_specs=in_specs, out_specs=out_specs, check_vma=False)
```

```python
import functools
import math

import jax
import jax.numpy as jnp
from jax import lax
from jax.experimental import pallas as pl
from jax.experimental.pallas import tpu as pltpu
from jax.sharding import PartitionSpec as P


BF16 = jnp.bfloat16
F32 = jnp.float32


def tables(length):
    counter = jnp.arange(length, dtype=jnp.int32)
    product = counter[:, None] * counter[None, :] % length
    angles = product.astype(F32) * (2.0 * math.pi / length)
    return jnp.cos(angles).astype(BF16), jnp.sin(angles).astype(BF16)


def block_tables(length):
    cosine, sine = tables(length)
    left = jnp.concatenate(
        [jnp.concatenate([cosine, sine], 1), jnp.concatenate([-sine, cosine], 1)], 0
    )
    right = jnp.concatenate(
        [jnp.concatenate([cosine, -sine], 1), jnp.concatenate([sine, cosine], 1)], 0
    )
    return left, right


def dot(left_side, right_side):
    return jnp.dot(left_side, right_side, preferred_element_type=F32)


def cost(flops, moved):
    return pl.CostEstimate(flops=int(flops), bytes_accessed=int(moved), transcendentals=0)


def spec(shape, index=None):
    rank = len(shape)
    return pl.BlockSpec(shape, index or (lambda *_: (0,) * rank))


SCALARS = pl.BlockSpec(memory_space=pltpu.SMEM)
WHOLE = pl.BlockSpec(memory_space=pltpu.VMEM)
UNROLL = 8
LANES = 128


def column_row(cols_ref, owner, count):
    return cols_ref[:, pl.ds(pl.multiple_of(owner * count, LANES), count)]


def flip(cols, ny, nz):
    return lax.rem(ny - cols // nz, ny) * nz + lax.rem(nz - cols % nz, nz)


def one_hot(row, base, size):
    position = lax.broadcasted_iota(jnp.int32, (size, row.shape[1]), 0) + base
    return jnp.where(row == position, 1.0, 0.0).astype(BF16)


def dot_t(left_side, right_side):
    dims = (((1,), (1,)), ((), ()))
    return lax.dot_general(left_side, right_side, dims, preferred_element_type=F32)


def mirror_kernel(span, nz, me_ref, kernel_ref, cols_ref, out_ref, first_ref):
    nx, count = kernel_ref.shape
    row = lax.broadcasted_iota(jnp.int32, (nx, nx), 0)
    column = lax.broadcasted_iota(jnp.int32, (nx, nx), 1)
    swap = jnp.where(lax.rem(row + column, nx) == 0, 1.0, 0.0).astype(BF16)
    mirrored = dot(swap, kernel_ref[...].astype(BF16)).astype(BF16)
    out_ref[...] = mirrored
    local_cols = column_row(cols_ref, me_ref[0], count) - me_ref[0] * span
    target = jnp.where(local_cols < nz, lax.rem(nz - local_cols, nz), -1)
    first_ref[...] = dot_t(mirrored, one_hot(target, 0, nz)).astype(BF16)


def mirror(me, kernel, cols, span, nz):
    nx = kernel.shape[0]
    return pl.pallas_call(
        functools.partial(mirror_kernel, span, nz),
        out_shape=[jax.ShapeDtypeStruct(kernel.shape, BF16), jax.ShapeDtypeStruct((nx, nz), BF16)],
        in_specs=[SCALARS, WHOLE, WHOLE],
        out_specs=[WHOLE] * 2,
        cost_estimate=cost(2 * nx * nx * kernel.shape[1], 6 * kernel.size),
        name="mirror",
    )(me, kernel, cols)


def expand_kernel(scale, groups, span, ny, me_ref, own_ref, neg_ref, first_ref, cols_ref, out_ref, hot):
    nx, count = own_ref.shape
    length = out_ref.shape[2]
    wide = 2 * length
    me = me_ref[0]
    both = jnp.concatenate([own_ref[...].astype(BF16), neg_ref[...]], 1)
    mine = column_row(cols_ref, me, count) - me * span
    theirs = flip(column_row(cols_ref, groups - 1 - me, count), ny, length) - me * span
    group = jnp.concatenate([mine, theirs + span], 1) // wide
    group = group - jnp.concatenate(
        [jnp.zeros((1, count), jnp.int32), jnp.full((1, count), span // wide, jnp.int32)], 1
    )
    hot[:, :count] = one_hot(mine & (wide - 1), 0, wide)
    hot[:, count:] = one_hot(theirs & (wide - 1), 0, wide)

    def step(number, carry):
        sides = []
        for k in range(2):
            wanted = jnp.where(group == 2 * number + k, 1.0, 0.0).astype(BF16)
            sides.append(both * wanted)
        total = dot_t(jnp.concatenate(sides, 0), hot[...])
        for k in range(2):
            for half in range(2):
                out_ref[4 * number + 2 * k + half] = (
                    total[k * nx : (k + 1) * nx, half * length : (half + 1) * length] * scale
                )
        return carry

    lax.fori_loop(0, out_ref.shape[0] // 4, step, 0)
    out_ref[0] = out_ref[0] + first_ref[...].astype(F32) * scale


def expand(me, kernel, neg, first, cols, groups, ny, length, scale):
    nx, count = kernel.shape
    rows = ny // groups
    return pl.pallas_call(
        functools.partial(expand_kernel, scale, groups, rows * length, ny),
        out_shape=jax.ShapeDtypeStruct((rows, nx, length), F32),
        in_specs=[SCALARS] + [WHOLE] * 4,
        out_specs=WHOLE,
        scratch_shapes=[pltpu.VMEM((2 * length, 2 * count), BF16)],
        cost_estimate=cost(4 * nx * count * rows * length, 4 * nx * (count + rows * length)),
        name="expand",
    )(me, kernel, neg, first, cols)


def forward_kernel(parts, base, cuts, me_ref, grid_ref, own_ref, *refs):
    piece_refs = refs[:parts]
    if parts > 1:
        zt_ref, yt_ref, their_ref = refs[parts : parts + 3]
        per = piece_refs[0].shape[0]
        for slot, piece_ref in enumerate(piece_refs):
            their_ref[pl.ds((me_ref[0] ^ slot) * per, per)] = piece_ref[...]
    else:
        their_ref, zt_ref, yt_ref = refs[:3]
    out_refs, hold = refs[3 + parts - (parts == 1) : -1], refs[-1]
    count, ny, nz = own_ref.shape[1:]
    tiles = ny // their_ref.shape[1]
    zt, yt = zt_ref[...], yt_ref[...]

    def step(pair, carry):
        lines = []
        for k in range(2):
            x = 2 * pair + k
            theirs = their_ref[pl.ds((base + x) * tiles, tiles)].reshape(ny, nz)
            lines.append(jnp.concatenate([own_ref[0, x] * theirs, own_ref[1, x] * theirs], 1))
        first = dot(jnp.concatenate(lines, 0), zt).astype(BF16)
        stack = jnp.concatenate(
            [
                jnp.concatenate([first[:ny, :nz], first[ny:, :nz]], 1),
                jnp.concatenate([first[:ny, nz:], first[ny:, nz:]], 1),
            ],
            0,
        )
        second = dot(yt, stack)
        for k in range(2):
            for c in range(2):
                hold[c, pl.ds(2 * pair + k, ny, stride=count), :] = second[
                    c * ny : (c + 1) * ny, k * nz : (k + 1) * nz
                ]
        return carry

    lax.fori_loop(0, count // 2, step, 0, unroll=min(UNROLL, count // 2))
    part = ny // len(out_refs)
    for number, out_ref in enumerate(out_refs):
        owner = grid_ref[0] ^ (number // cuts)
        begin = (owner * cuts + number % cuts) * (part * count)
        for c in range(2):
            piece = hold[c, pl.ds(begin, part * count), :]
            out_ref[:, c] = piece.astype(BF16).reshape(part, count, nz)


def forward(me, grid_pos, own, pieces, half, count, zt, yt, groups, cuts):
    ny, nz = own.shape[2:]
    part = ny // (groups * cuts)
    parts = len(pieces)
    shape = jax.ShapeDtypeStruct((part, 2, count, nz), BF16)
    their = jax.ShapeDtypeStruct((parts * pieces[0].shape[0],) + pieces[0].shape[1:], BF16)
    outs = ([their] if parts > 1 else []) + [shape] * (groups * cuts)
    return pl.pallas_call(
        functools.partial(forward_kernel, parts, half * count, cuts),
        grid=(1,),
        out_shape=outs,
        in_specs=[SCALARS, SCALARS, spec((2, count, ny, nz), lambda i: (0, half, 0, 0))]
        + [spec(p.shape) for p in pieces]
        + [spec(zt.shape), spec(yt.shape)],
        out_specs=[spec(o.shape) for o in outs],
        scratch_shapes=[pltpu.VMEM((2, ny * count, nz), F32)],
        cost_estimate=cost(2 * count * ny * nz * 2 * (2 * ny + 2 * nz), 12 * count * ny * nz),
        name="forward",
    )(me, grid_pos, own, *pieces, zt, yt)


def middle_kernel(groups, halves, grid_ref, *refs):
    in_refs = refs[:groups]
    kern_ref, xt_ref, ixt_ref = refs[groups : groups + 3]
    out_refs, hold = refs[groups + 3 : -1], refs[-1]
    count, nx, nz = kern_ref.shape
    xt, ixt = xt_ref[...], ixt_ref[...]

    def step(pair, carry):
        lines, factors = [], []
        for k in range(2):
            line = 2 * pair + k
            lines.append(jnp.concatenate([r[line, c] for c in range(2) for r in in_refs], 0))
            factors.append(kern_ref[line])
        factor = jnp.concatenate(factors, 1)
        spectrum = dot(xt, jnp.concatenate(lines, 1))
        scaled = jnp.concatenate(
            [(spectrum[:nx] * factor).astype(BF16), (spectrum[nx:] * factor).astype(BF16)], 0
        )
        third = dot(ixt, scaled)
        for k in range(2):
            for c in range(2):
                hold[c, pl.ds(2 * pair + k, nx, stride=count), :] = third[
                    c * nx : (c + 1) * nx, k * nz : (k + 1) * nz
                ]
        return carry

    lax.fori_loop(0, count // 2, step, 0, unroll=min(UNROLL, count // 2))
    rows = nx // (groups * halves)
    for number, out_ref in enumerate(out_refs):
        owner = grid_ref[0] ^ (number // halves)
        begin = (owner * halves + number % halves) * (rows * count)
        for c in range(2):
            piece = hold[c, pl.ds(begin, rows * count), :]
            out_ref[:, c] = piece.astype(BF16).reshape(rows, count, nz)


def middle(grid_pos, pieces, kern, cut, xt, ixt, halves):
    groups = len(pieces)
    count, nx, nz = pieces[0].shape[0], kern.shape[1], kern.shape[2]
    rows = nx // (groups * halves)
    shape = jax.ShapeDtypeStruct((rows, 2, count, nz), BF16)
    return pl.pallas_call(
        functools.partial(middle_kernel, groups, halves),
        grid=(1,),
        out_shape=[shape] * (groups * halves),
        in_specs=[SCALARS]
        + [spec(p.shape) for p in pieces]
        + [spec((count, nx, nz), lambda i: (cut, 0, 0)), spec(xt.shape), spec(ixt.shape)],
        out_specs=[spec(shape.shape)] * (groups * halves),
        scratch_shapes=[pltpu.VMEM((2, nx * count, nz), F32)],
        cost_estimate=cost(16 * nx * nx * count * nz, 12 * count * nx * nz),
        name="middle",
    )(grid_pos, *pieces, kern, xt, ixt)


def backward_kernel(bases, has_total, base, *refs):
    in_refs = refs[: len(bases)]
    their_ref, weight_ref, yt_ref, zt_ref = refs[len(bases) : len(bases) + 4]
    total_ref = refs[len(bases) + 4] if has_total == 2 else None
    out_ref = refs[-1]
    count, ny, nz = out_ref.shape[1:]
    tiles = ny // their_ref.shape[1]
    zt, yt = zt_ref[...], yt_ref[...]
    weight = weight_ref[0]

    def step(pair, carry):
        lines = []
        for k in range(2):
            x = 2 * pair + k
            lines.append(jnp.concatenate([r[x + b, c] for c in range(2) for r, b in zip(in_refs, bases)], 0))
        fourth = dot(yt, jnp.concatenate(lines, 1)).astype(BF16)
        stack = jnp.concatenate(
            [
                jnp.concatenate([fourth[:ny, k * nz : (k + 1) * nz], fourth[ny:, k * nz : (k + 1) * nz]], 1)
                for k in range(2)
            ],
            0,
        )
        potential = dot(stack, zt)
        for k in range(2):
            x = 2 * pair + k
            theirs = their_ref[pl.ds((base + x) * tiles, tiles)].reshape(ny, nz).astype(F32) * weight
            for n in range(2):
                term = potential[k * ny : (k + 1) * ny, n * nz : (n + 1) * nz] * theirs
                if total_ref is None:
                    out_ref[n, x] = -term
                else:
                    out_ref[n, x] = total_ref[n, x] - term
        return carry

    lax.fori_loop(0, count // 2, step, 0, unroll=min(UNROLL, count // 2))


def backward(pieces, bases, their, weight, yt, zt, total, accumulate, part_number, count, slab):
    ny, nz = sum(p.shape[2] for p in pieces), pieces[0].shape[3]
    number = len(pieces)
    block = spec((2, count, ny, nz), lambda i: (0, part_number, 0, 0))
    has_total = 0 if total is None else (2 if accumulate else 1)
    extra = [] if total is None else [total]
    extra_specs = [] if total is None else [block if accumulate else pl.BlockSpec(memory_space=pl.ANY)]
    return pl.pallas_call(
        functools.partial(backward_kernel, bases, has_total, part_number * count),
        grid=(1,),
        out_shape=jax.ShapeDtypeStruct((2, slab, ny, nz), F32),
        in_specs=[spec(p.shape) for p in pieces]
        + [spec(their.shape), SCALARS, spec(yt.shape), spec(zt.shape)]
        + extra_specs,
        out_specs=block,
        input_output_aliases={number + 4: 0} if extra else {},
        cost_estimate=cost(2 * count * ny * nz * 2 * (2 * ny + 2 * nz), 24 * count * ny * nz),
        name="backward",
    )(*pieces, their, weight, yt, zt, *extra)


TILE = 16


def after(value, *others):
    return lax.optimization_barrier((value, others))[0]


def shift(value, axis, size, mask):
    return lax.ppermute(value, axis, [(i, i ^ mask) for i in range(size)]) if mask else value


def split_kernel(me_ref, in_ref, *out_refs):
    per = out_refs[0].shape[0]
    for slot, out_ref in enumerate(out_refs):
        out_ref[...] = in_ref[0, pl.ds((me_ref[0] ^ slot) * per, per)]


def split(me, value, band, chunk, tiles, parts):
    shape = jax.ShapeDtypeStruct((tiles // parts,) + value.shape[2:], value.dtype)
    return pl.pallas_call(
        split_kernel,
        grid=(1,),
        out_shape=[shape] * parts,
        in_specs=[SCALARS, spec((1, tiles) + value.shape[2:], lambda i: (band, chunk, 0, 0))],
        out_specs=[spec(shape.shape)] * parts,
        cost_estimate=cost(0, 4 * tiles * TILE * value.shape[3]),
        name="split",
    )(me, value)


def pick_kernel(parts, choice_ref, *refs):
    in_refs, out_refs, hold = refs[:parts], refs[parts:-1], refs[-1]
    for slot, in_ref in enumerate(in_refs):
        hold[slot] = in_ref[...]
    for slot, out_ref in enumerate(out_refs):
        out_ref[...] = hold[choice_ref[slot]]


def pick(choice, pieces):
    parts, shape = len(pieces), pieces[0].shape
    return pl.pallas_call(
        functools.partial(pick_kernel, parts),
        out_shape=[jax.ShapeDtypeStruct(shape, pieces[0].dtype)] * parts,
        in_specs=[SCALARS] + [WHOLE] * parts,
        out_specs=[WHOLE] * parts,
        scratch_shapes=[pltpu.VMEM((parts,) + shape, pieces[0].dtype)],
        cost_estimate=cost(0, 4 * parts * math.prod(shape)),
        name="pick",
    )(choice, *pieces)


def pick_stacked_kernel(parts, choice_ref, *refs):
    in_refs, out_ref, hold = refs[:parts], refs[-2], refs[-1]
    for slot, in_ref in enumerate(in_refs):
        hold[slot] = in_ref[...]
    for number in range(parts):
        out_ref[number] = hold[choice_ref[number]]


def pick_stacked(choice, pieces):
    parts, shape = len(pieces), pieces[0].shape
    return pl.pallas_call(
        functools.partial(pick_stacked_kernel, parts),
        out_shape=jax.ShapeDtypeStruct((parts,) + shape, pieces[0].dtype),
        in_specs=[SCALARS] + [WHOLE] * parts,
        out_specs=WHOLE,
        scratch_shapes=[pltpu.VMEM((parts,) + shape, pieces[0].dtype)],
        cost_estimate=cost(0, 4 * parts * math.prod(shape)),
        name="pick",
    )(choice, *pieces)


def local(orbitals, occupation, partner, col_index, kernel):
    bands, groups = lax.axis_size("band"), lax.axis_size("grid")
    slab, ny, nz = orbitals.shape[1:]
    nx, _ = kernel.shape
    lines = ny // groups
    band_pos, me = lax.axis_index("band"), lax.axis_index("grid")
    band_slots = jnp.arange(bands, dtype=jnp.int32)
    my_band = band_pos.astype(jnp.int32).reshape(1)
    choice = jnp.take(partner, band_slots ^ band_pos) ^ band_pos
    pick_choice = partner ^ band_pos
    tiled = orbitals.reshape(2, slab * ny // TILE, TILE, nz)

    def swap(value, slot):
        return shift(value, "grid", groups, slot)

    def exchange(value):
        return lax.all_to_all(value, "band", split_axis=0, concat_axis=0, tiled=True)

    def slotwise(sent):
        return [shift(piece, "band", bands, slot) for slot, piece in enumerate(sent)]

    my_grid = me.astype(jnp.int32).reshape(1)
    cols = col_index.reshape(1, -1)
    sent = split(my_band, tiled, 0, 0, slab * ny // TILE, bands)
    arrived = slotwise(sent)
    sent1 = split(my_band, after(tiled, *sent), 1, 0, slab * ny // TILE, bands)

    mirror_of = [(i, groups - 1 - i) for i in range(groups)]
    mirror_first = [(i, (groups - i) % groups) for i in range(groups)]
    mirrored, first_line = mirror(my_grid, after(kernel, *sent), cols, lines * nz, nz)
    neg = lax.ppermute(mirrored, "grid", mirror_of)
    first = lax.ppermute(first_line, "grid", mirror_first)

    def slots(table, axis):
        shape = table.shape
        blocks = table.reshape(shape[:axis] + (2, groups, shape[axis] // (2 * groups)) + shape[axis + 1 :])
        order = jnp.arange(groups, dtype=jnp.int32) ^ me
        return jnp.take(blocks, order, axis=axis + 1).reshape(shape)

    xleft, xright = block_tables(nx)
    yleft, yright = block_tables(ny)
    zleft, zright = block_tables(nz)
    x_forward, y_inverse = slots(xleft, 1), slots(yright, 1)
    cuts = 2 if lines % 32 == 0 else 1
    parts = 2 if slab % 32 == 0 else 1

    picked = pick(choice, after(arrived, mirrored, first_line, *sent1))
    fetched = slotwise(picked)
    arrived = slotwise(after(sent1, *picked))

    def outward(pieces):
        outs = forward(my_band, my_grid, orbitals, pieces, 0, slab, zright, yleft, groups, cuts)
        their, sent = (outs[0], outs[1:]) if len(pieces) > 1 else (pieces[0], outs)
        moved = [
            [swap(sent[slot * cuts + cut], slot) for slot in range(groups)]
            for cut in range(cuts)
        ]
        return their, sent, moved

    their0, sent, moved0 = outward(fetched)
    picked = pick_stacked(pick_choice, after(arrived, *sent))
    their1 = exchange(picked.reshape(tiled.shape[1:]))
    kern = expand(
        my_grid, after(kernel, picked), neg, first, cols, groups, ny, nz, 0.5 / (nx * ny * nz)
    )

    def inward(moved, halves):
        answers, back = [], []
        for cut in range(cuts):
            answers.append(middle(my_grid, moved[cut], kern, cut, x_forward, xright, halves[cut]))
            back.append([
                swap(value, number // halves[cut])
                for number, value in enumerate(answers[cut])
            ])
        split_rows = max(halves)
        result = []
        for h in range(split_rows):
            pieces, bases = [], []
            for slot in range(groups):
                for cut in range(cuts):
                    whole = halves[cut] == 1
                    pieces.append(back[cut][slot if whole else slot * halves[cut] + h])
                    bases.append(h * (slab // split_rows) if whole else 0)
            result.append((pieces, bases))
        return answers, result

    answers0, back0 = inward(moved0, (1,) * cuts)
    their1, _, moved1 = outward([after(their1, *answers0[-1])])
    _, back1 = inward(moved1, (1,) * (cuts - 1) + (parts,))

    def weight(m):
        return lax.dynamic_slice_in_dim(occupation, partner[band_pos] * 2 + m, 1, 0)

    pieces, bases = back0[0]
    total = backward(pieces, bases, their0, weight(0), y_inverse, zleft, None, False, 0, slab, slab)
    for h, (pieces, bases) in enumerate(back1):
        total = backward(
            pieces, bases, their1, weight(1), y_inverse, zleft, total, True, h, slab // len(back1), slab
        )
    return total


def solution(mesh):
    in_specs = (P("band", "grid", None, None), P(), P(), P(), P(None, "grid"))
    out_specs = P("band", "grid", None, None)
    return jax.shard_map(local, mesh=mesh, in_specs=in_specs, out_specs=out_specs, check_vma=False)
```

```python
import functools
import math

import jax
import jax.numpy as jnp
from jax import lax
from jax.experimental import pallas as pl
from jax.experimental.pallas import tpu as pltpu
from jax.sharding import PartitionSpec as P


BF16 = jnp.bfloat16
F32 = jnp.float32


def tables(length):
    counter = jnp.arange(length, dtype=jnp.int32)
    product = counter[:, None] * counter[None, :] % length
    angles = product.astype(F32) * (2.0 * math.pi / length)
    return jnp.cos(angles).astype(BF16), jnp.sin(angles).astype(BF16)


def block_tables(length):
    cosine, sine = tables(length)
    left = jnp.concatenate(
        [jnp.concatenate([cosine, sine], 1), jnp.concatenate([-sine, cosine], 1)], 0
    )
    right = jnp.concatenate(
        [jnp.concatenate([cosine, -sine], 1), jnp.concatenate([sine, cosine], 1)], 0
    )
    return left, right


def dot(left_side, right_side):
    return jnp.dot(left_side, right_side, preferred_element_type=F32)


def cost(flops, moved):
    return pl.CostEstimate(flops=int(flops), bytes_accessed=int(moved), transcendentals=0)


def spec(shape, index=None):
    rank = len(shape)
    return pl.BlockSpec(shape, index or (lambda *_: (0,) * rank))


SCALARS = pl.BlockSpec(memory_space=pltpu.SMEM)
WHOLE = pl.BlockSpec(memory_space=pltpu.VMEM)
UNROLL = 8
LANES = 128


def column_row(cols_ref, owner, count):
    return cols_ref[:, pl.ds(pl.multiple_of(owner * count, LANES), count)]


def flip(cols, ny, nz):
    return lax.rem(ny - cols // nz, ny) * nz + lax.rem(nz - cols % nz, nz)


def one_hot(row, base, size):
    position = lax.broadcasted_iota(jnp.int32, (size, row.shape[1]), 0) + base
    return jnp.where(row == position, 1.0, 0.0).astype(BF16)


def dot_t(left_side, right_side):
    dims = (((1,), (1,)), ((), ()))
    return lax.dot_general(left_side, right_side, dims, preferred_element_type=F32)


def mirror_kernel(span, nz, me_ref, kernel_ref, cols_ref, out_ref, first_ref):
    nx, count = kernel_ref.shape
    row = lax.broadcasted_iota(jnp.int32, (nx, nx), 0)
    column = lax.broadcasted_iota(jnp.int32, (nx, nx), 1)
    swap = jnp.where(lax.rem(row + column, nx) == 0, 1.0, 0.0).astype(BF16)
    mirrored = dot(swap, kernel_ref[...].astype(BF16)).astype(BF16)
    out_ref[...] = mirrored
    local_cols = column_row(cols_ref, me_ref[0], count) - me_ref[0] * span
    target = jnp.where(local_cols < nz, lax.rem(nz - local_cols, nz), -1)
    first_ref[...] = dot_t(mirrored, one_hot(target, 0, nz)).astype(BF16)


def mirror(me, kernel, cols, span, nz):
    nx = kernel.shape[0]
    return pl.pallas_call(
        functools.partial(mirror_kernel, span, nz),
        out_shape=[jax.ShapeDtypeStruct(kernel.shape, BF16), jax.ShapeDtypeStruct((nx, nz), BF16)],
        in_specs=[SCALARS, WHOLE, WHOLE],
        out_specs=[WHOLE] * 2,
        cost_estimate=cost(2 * nx * nx * kernel.shape[1], 6 * kernel.size),
        name="mirror",
    )(me, kernel, cols)


def expand_kernel(scale, groups, span, ny, me_ref, own_ref, neg_ref, first_ref, cols_ref, out_ref, hot):
    nx, count = own_ref.shape
    length = out_ref.shape[2]
    wide = 2 * length
    me = me_ref[0]
    both = jnp.concatenate([own_ref[...].astype(BF16), neg_ref[...]], 1)
    mine = column_row(cols_ref, me, count) - me * span
    theirs = flip(column_row(cols_ref, groups - 1 - me, count), ny, length) - me * span
    group = jnp.concatenate([mine, theirs + span], 1) // wide
    group = group - jnp.concatenate(
        [jnp.zeros((1, count), jnp.int32), jnp.full((1, count), span // wide, jnp.int32)], 1
    )
    hot[:, :count] = one_hot(mine & (wide - 1), 0, wide)
    hot[:, count:] = one_hot(theirs & (wide - 1), 0, wide)

    def step(number, carry):
        sides = []
        for k in range(2):
            wanted = jnp.where(group == 2 * number + k, 1.0, 0.0).astype(BF16)
            sides.append(both * wanted)
        total = dot_t(jnp.concatenate(sides, 0), hot[...])
        for k in range(2):
            for half in range(2):
                out_ref[4 * number + 2 * k + half] = (
                    total[k * nx : (k + 1) * nx, half * length : (half + 1) * length] * scale
                )
        return carry

    lax.fori_loop(0, out_ref.shape[0] // 4, step, 0)
    out_ref[0] = out_ref[0] + first_ref[...].astype(F32) * scale


def expand(me, kernel, neg, first, cols, groups, ny, length, scale):
    nx, count = kernel.shape
    rows = ny // groups
    return pl.pallas_call(
        functools.partial(expand_kernel, scale, groups, rows * length, ny),
        out_shape=jax.ShapeDtypeStruct((rows, nx, length), F32),
        in_specs=[SCALARS] + [WHOLE] * 4,
        out_specs=WHOLE,
        scratch_shapes=[pltpu.VMEM((2 * length, 2 * count), BF16)],
        cost_estimate=cost(4 * nx * count * rows * length, 4 * nx * (count + rows * length)),
        name="expand",
    )(me, kernel, neg, first, cols)


def forward_kernel(parts, base, cuts, me_ref, grid_ref, own_ref, *refs):
    piece_refs = refs[:parts]
    if parts > 1:
        zt_ref, yt_ref, their_ref = refs[parts : parts + 3]
        per = piece_refs[0].shape[0]
        for slot, piece_ref in enumerate(piece_refs):
            their_ref[pl.ds((me_ref[0] ^ slot) * per, per)] = piece_ref[...]
    else:
        their_ref, zt_ref, yt_ref = refs[:3]
    out_refs, hold = refs[3 + parts - (parts == 1) : -1], refs[-1]
    count, ny, nz = own_ref.shape[1:]
    tiles = ny // their_ref.shape[1]
    zt, yt = zt_ref[...], yt_ref[...]

    def step(pair, carry):
        lines = []
        for k in range(2):
            x = 2 * pair + k
            theirs = their_ref[pl.ds((base + x) * tiles, tiles)].reshape(ny, nz)
            lines.append(jnp.concatenate([own_ref[0, x] * theirs, own_ref[1, x] * theirs], 1))
        first = dot(jnp.concatenate(lines, 0), zt).astype(BF16)
        stack = jnp.concatenate(
            [
                jnp.concatenate([first[:ny, :nz], first[ny:, :nz]], 1),
                jnp.concatenate([first[:ny, nz:], first[ny:, nz:]], 1),
            ],
            0,
        )
        second = dot(yt, stack)
        for k in range(2):
            for c in range(2):
                hold[c, pl.ds(2 * pair + k, ny, stride=count), :] = second[
                    c * ny : (c + 1) * ny, k * nz : (k + 1) * nz
                ]
        return carry

    lax.fori_loop(0, count // 2, step, 0, unroll=min(UNROLL, count // 2))
    part = ny // len(out_refs)
    for number, out_ref in enumerate(out_refs):
        owner = grid_ref[0] ^ (number // cuts)
        begin = (owner * cuts + number % cuts) * (part * count)
        for c in range(2):
            piece = hold[c, pl.ds(begin, part * count), :]
            out_ref[:, c] = piece.astype(BF16).reshape(part, count, nz)


def forward(me, grid_pos, own, pieces, half, count, zt, yt, groups, cuts):
    ny, nz = own.shape[2:]
    part = ny // (groups * cuts)
    parts = len(pieces)
    shape = jax.ShapeDtypeStruct((part, 2, count, nz), BF16)
    their = jax.ShapeDtypeStruct((parts * pieces[0].shape[0],) + pieces[0].shape[1:], BF16)
    outs = ([their] if parts > 1 else []) + [shape] * (groups * cuts)
    return pl.pallas_call(
        functools.partial(forward_kernel, parts, half * count, cuts),
        grid=(1,),
        out_shape=outs,
        in_specs=[SCALARS, SCALARS, spec((2, count, ny, nz), lambda i: (0, half, 0, 0))]
        + [spec(p.shape) for p in pieces]
        + [spec(zt.shape), spec(yt.shape)],
        out_specs=[spec(o.shape) for o in outs],
        scratch_shapes=[pltpu.VMEM((2, ny * count, nz), F32)],
        cost_estimate=cost(2 * count * ny * nz * 2 * (2 * ny + 2 * nz), 12 * count * ny * nz),
        name="forward",
    )(me, grid_pos, own, *pieces, zt, yt)


def middle_kernel(groups, halves, grid_ref, *refs):
    in_refs = refs[:groups]
    kern_ref, xt_ref, ixt_ref = refs[groups : groups + 3]
    out_refs, hold = refs[groups + 3 : -1], refs[-1]
    count, nx, nz = kern_ref.shape
    xt, ixt = xt_ref[...], ixt_ref[...]

    def step(pair, carry):
        lines, factors = [], []
        for k in range(2):
            line = 2 * pair + k
            lines.append(jnp.concatenate([r[line, c] for c in range(2) for r in in_refs], 0))
            factors.append(kern_ref[line])
        factor = jnp.concatenate(factors, 1)
        spectrum = dot(xt, jnp.concatenate(lines, 1))
        scaled = jnp.concatenate(
            [(spectrum[:nx] * factor).astype(BF16), (spectrum[nx:] * factor).astype(BF16)], 0
        )
        third = dot(ixt, scaled)
        for k in range(2):
            for c in range(2):
                hold[c, pl.ds(2 * pair + k, nx, stride=count), :] = third[
                    c * nx : (c + 1) * nx, k * nz : (k + 1) * nz
                ]
        return carry

    lax.fori_loop(0, count // 2, step, 0, unroll=min(UNROLL, count // 2))
    rows = nx // (groups * halves)
    for number, out_ref in enumerate(out_refs):
        owner = grid_ref[0] ^ (number // halves)
        begin = (owner * halves + number % halves) * (rows * count)
        for c in range(2):
            piece = hold[c, pl.ds(begin, rows * count), :]
            out_ref[:, c] = piece.astype(BF16).reshape(rows, count, nz)


def middle(grid_pos, pieces, kern, cut, xt, ixt, halves):
    groups = len(pieces)
    count, nx, nz = pieces[0].shape[0], kern.shape[1], kern.shape[2]
    rows = nx // (groups * halves)
    shape = jax.ShapeDtypeStruct((rows, 2, count, nz), BF16)
    return pl.pallas_call(
        functools.partial(middle_kernel, groups, halves),
        grid=(1,),
        out_shape=[shape] * (groups * halves),
        in_specs=[SCALARS]
        + [spec(p.shape) for p in pieces]
        + [spec((count, nx, nz), lambda i: (cut, 0, 0)), spec(xt.shape), spec(ixt.shape)],
        out_specs=[spec(shape.shape)] * (groups * halves),
        scratch_shapes=[pltpu.VMEM((2, nx * count, nz), F32)],
        cost_estimate=cost(16 * nx * nx * count * nz, 12 * count * nx * nz),
        name="middle",
    )(grid_pos, *pieces, kern, xt, ixt)


def backward_kernel(bases, has_total, base, *refs):
    in_refs = refs[: len(bases)]
    their_ref, weight_ref, yt_ref, zt_ref = refs[len(bases) : len(bases) + 4]
    total_ref = refs[len(bases) + 4] if has_total == 2 else None
    out_ref = refs[-1]
    count, ny, nz = out_ref.shape[1:]
    tiles = ny // their_ref.shape[1]
    zt, yt = zt_ref[...], yt_ref[...]
    weight = weight_ref[0]

    def step(pair, carry):
        lines = []
        for k in range(2):
            x = 2 * pair + k
            lines.append(jnp.concatenate([r[x + b, c] for c in range(2) for r, b in zip(in_refs, bases)], 0))
        fourth = dot(yt, jnp.concatenate(lines, 1)).astype(BF16)
        stack = jnp.concatenate(
            [
                jnp.concatenate([fourth[:ny, k * nz : (k + 1) * nz], fourth[ny:, k * nz : (k + 1) * nz]], 1)
                for k in range(2)
            ],
            0,
        )
        potential = dot(stack, zt)
        for k in range(2):
            x = 2 * pair + k
            theirs = their_ref[pl.ds((base + x) * tiles, tiles)].reshape(ny, nz).astype(F32) * weight
            for n in range(2):
                term = potential[k * ny : (k + 1) * ny, n * nz : (n + 1) * nz] * theirs
                if total_ref is None:
                    out_ref[n, x] = -term
                else:
                    out_ref[n, x] = total_ref[n, x] - term
        return carry

    lax.fori_loop(0, count // 2, step, 0, unroll=min(UNROLL, count // 2))


def backward(pieces, bases, their, weight, yt, zt, total, accumulate, part_number, count, slab):
    ny, nz = sum(p.shape[2] for p in pieces), pieces[0].shape[3]
    number = len(pieces)
    block = spec((2, count, ny, nz), lambda i: (0, part_number, 0, 0))
    has_total = 0 if total is None else (2 if accumulate else 1)
    extra = [] if total is None else [total]
    extra_specs = [] if total is None else [block if accumulate else pl.BlockSpec(memory_space=pl.ANY)]
    return pl.pallas_call(
        functools.partial(backward_kernel, bases, has_total, part_number * count),
        grid=(1,),
        out_shape=jax.ShapeDtypeStruct((2, slab, ny, nz), F32),
        in_specs=[spec(p.shape) for p in pieces]
        + [spec(their.shape), SCALARS, spec(yt.shape), spec(zt.shape)]
        + extra_specs,
        out_specs=block,
        input_output_aliases={number + 4: 0} if extra else {},
        cost_estimate=cost(2 * count * ny * nz * 2 * (2 * ny + 2 * nz), 24 * count * ny * nz),
        name="backward",
    )(*pieces, their, weight, yt, zt, *extra)


TILE = 16


def after(value, *others):
    return lax.optimization_barrier((value, others))[0]


def shift(value, axis, size, mask):
    return lax.ppermute(value, axis, [(i, i ^ mask) for i in range(size)]) if mask else value


def split_kernel(me_ref, in_ref, *out_refs):
    per = out_refs[0].shape[0]
    for slot, out_ref in enumerate(out_refs):
        out_ref[...] = in_ref[0, pl.ds((me_ref[0] ^ slot) * per, per)]


def split(me, value, band, chunk, tiles, parts):
    shape = jax.ShapeDtypeStruct((tiles // parts,) + value.shape[2:], value.dtype)
    return pl.pallas_call(
        split_kernel,
        grid=(1,),
        out_shape=[shape] * parts,
        in_specs=[SCALARS, spec((1, tiles) + value.shape[2:], lambda i: (band, chunk, 0, 0))],
        out_specs=[spec(shape.shape)] * parts,
        cost_estimate=cost(0, 4 * tiles * TILE * value.shape[3]),
        name="split",
    )(me, value)


def pick_kernel(parts, choice_ref, *refs):
    in_refs, out_refs, hold = refs[:parts], refs[parts:-1], refs[-1]
    for slot, in_ref in enumerate(in_refs):
        hold[slot] = in_ref[...]
    for slot, out_ref in enumerate(out_refs):
        out_ref[...] = hold[choice_ref[slot]]


def pick(choice, pieces):
    parts, shape = len(pieces), pieces[0].shape
    return pl.pallas_call(
        functools.partial(pick_kernel, parts),
        out_shape=[jax.ShapeDtypeStruct(shape, pieces[0].dtype)] * parts,
        in_specs=[SCALARS] + [WHOLE] * parts,
        out_specs=[WHOLE] * parts,
        scratch_shapes=[pltpu.VMEM((parts,) + shape, pieces[0].dtype)],
        cost_estimate=cost(0, 4 * parts * math.prod(shape)),
        name="pick",
    )(choice, *pieces)


def pick_stacked_kernel(parts, choice_ref, *refs):
    in_refs, out_ref, hold = refs[:parts], refs[-2], refs[-1]
    for slot, in_ref in enumerate(in_refs):
        hold[slot] = in_ref[...]
    for number in range(parts):
        out_ref[number] = hold[choice_ref[number]]


def pick_stacked(choice, pieces):
    parts, shape = len(pieces), pieces[0].shape
    return pl.pallas_call(
        functools.partial(pick_stacked_kernel, parts),
        out_shape=jax.ShapeDtypeStruct((parts,) + shape, pieces[0].dtype),
        in_specs=[SCALARS] + [WHOLE] * parts,
        out_specs=WHOLE,
        scratch_shapes=[pltpu.VMEM((parts,) + shape, pieces[0].dtype)],
        cost_estimate=cost(0, 4 * parts * math.prod(shape)),
        name="pick",
    )(choice, *pieces)


def local(orbitals, occupation, partner, col_index, kernel):
    bands, groups = lax.axis_size("band"), lax.axis_size("grid")
    slab, ny, nz = orbitals.shape[1:]
    nx, _ = kernel.shape
    lines = ny // groups
    band_pos, me = lax.axis_index("band"), lax.axis_index("grid")
    band_slots = jnp.arange(bands, dtype=jnp.int32)
    my_band = band_pos.astype(jnp.int32).reshape(1)
    choice = jnp.take(partner, band_slots ^ band_pos) ^ band_pos
    pick_choice = partner ^ band_pos
    tiled = orbitals.reshape(2, slab * ny // TILE, TILE, nz)

    def swap(value, slot):
        return shift(value, "grid", groups, slot)

    def exchange(value):
        return lax.all_to_all(value, "band", split_axis=0, concat_axis=0, tiled=True)

    def slotwise(sent):
        return [shift(piece, "band", bands, slot) for slot, piece in enumerate(sent)]

    my_grid = me.astype(jnp.int32).reshape(1)
    cols = col_index.reshape(1, -1)
    blocks = tiled[0].reshape(bands, -1, TILE, nz)
    sent = [
        lax.dynamic_index_in_dim(blocks, band_pos ^ slot, 0, keepdims=False) for slot in range(bands)
    ]
    arrived = slotwise(sent)
    sent1 = split(my_band, after(tiled, *sent), 1, 0, slab * ny // TILE, bands)

    mirror_of = [(i, groups - 1 - i) for i in range(groups)]
    mirror_first = [(i, (groups - i) % groups) for i in range(groups)]
    mirrored, first_line = mirror(my_grid, after(kernel, *sent), cols, lines * nz, nz)
    neg = lax.ppermute(mirrored, "grid", mirror_of)
    first = lax.ppermute(first_line, "grid", mirror_first)

    def slots(table, axis):
        shape = table.shape
        blocks = table.reshape(shape[:axis] + (2, groups, shape[axis] // (2 * groups)) + shape[axis + 1 :])
        order = jnp.arange(groups, dtype=jnp.int32) ^ me
        return jnp.take(blocks, order, axis=axis + 1).reshape(shape)

    xleft, xright = block_tables(nx)
    yleft, yright = block_tables(ny)
    zleft, zright = block_tables(nz)
    x_forward, y_inverse = slots(xleft, 1), slots(yright, 1)
    cuts = 2 if lines % 32 == 0 else 1
    parts = 2 if slab % 32 == 0 else 1

    picked = pick(choice, after(arrived, mirrored, first_line, *sent1))
    fetched = slotwise(picked)
    kern = expand(
        my_grid, after(kernel, *picked), neg, first, cols, groups, ny, nz, 0.5 / (nx * ny * nz)
    )
    arrived = slotwise(after(sent1, kern))

    def outward(pieces):
        outs = forward(my_band, my_grid, orbitals, pieces, 0, slab, zright, yleft, groups, cuts)
        their, sent = (outs[0], outs[1:]) if len(pieces) > 1 else (pieces[0], outs)
        moved = [[swap(sent[slot * cuts + cut], slot) for slot in range(groups)] for cut in range(cuts)]
        return their, sent, moved

    their0, sent, moved0 = outward(fetched)
    picked = pick_stacked(pick_choice, after(arrived, *sent))
    their1 = exchange(picked.reshape(tiled.shape[1:]))

    def centre(cut, moved, halves):
        return middle(my_grid, moved[cut], kern, cut, x_forward, xright, halves)

    def home(values):
        return [swap(value, slot) for slot, value in enumerate(values)]

    def ending(m, total, back, bases, h, count, their):
        weight = lax.dynamic_slice_in_dim(occupation, partner[band_pos] * 2 + m, 1, 0)
        pieces = [piece for by_cut in zip(*back) for piece in by_cut]
        return backward(
            pieces, bases * groups, their, weight, y_inverse, zleft, total, m > 0, h, count, slab
        )

    answers = [centre(cut, moved0, 1) for cut in range(cuts)]
    back0 = [home(answers[cut]) for cut in range(cuts)]
    their1, _, moved1 = outward([after(their1, *answers[-1])])

    last = cuts - 1
    answers = [centre(cut, moved1, parts if cut == last else 1) for cut in range(cuts)]
    early = [home(answers[cut]) for cut in range(last)]
    rows = slab // parts
    late = [answers[last][h::parts] for h in range(parts)]
    late[0] = home(late[0])
    total = None
    for h in range(parts):
        if h == parts - 1:
            back0[0] = after(back0[0], *answers[last])
        total = ending(0, total, back0, (h * rows,) * cuts, h, rows, their0)
    for h in range(1, parts):
        late[h] = home(after(late[h], total))
    for h in range(parts):
        bases = (h * rows,) * last + (0,)
        total = ending(1, total, early + [late[h]], bases, h, rows, their1)
    return total


def solution(mesh):
    in_specs = (P("band", "grid", None, None), P(), P(), P(), P(None, "grid"))
    out_specs = P("band", "grid", None, None)
    return jax.shard_map(local, mesh=mesh, in_specs=in_specs, out_specs=out_specs, check_vma=False)
```

```python
import functools
import math

import jax
import jax.numpy as jnp
from jax import lax
from jax.experimental import pallas as pl
from jax.experimental.pallas import tpu as pltpu
from jax.sharding import PartitionSpec as P


BF16 = jnp.bfloat16
F32 = jnp.float32


def tables(length):
    counter = jnp.arange(length, dtype=jnp.int32)
    product = counter[:, None] * counter[None, :] % length
    angles = product.astype(F32) * (2.0 * math.pi / length)
    return jnp.cos(angles).astype(BF16), jnp.sin(angles).astype(BF16)


def block_tables(length):
    cosine, sine = tables(length)
    left = jnp.concatenate(
        [jnp.concatenate([cosine, sine], 1), jnp.concatenate([-sine, cosine], 1)], 0
    )
    right = jnp.concatenate(
        [jnp.concatenate([cosine, -sine], 1), jnp.concatenate([sine, cosine], 1)], 0
    )
    return left, right


def dot(left_side, right_side):
    return jnp.dot(left_side, right_side, preferred_element_type=F32)


def cost(flops, moved):
    return pl.CostEstimate(flops=int(flops), bytes_accessed=int(moved), transcendentals=0)


def spec(shape, index=None):
    rank = len(shape)
    return pl.BlockSpec(shape, index or (lambda *_: (0,) * rank))


SCALARS = pl.BlockSpec(memory_space=pltpu.SMEM)
WHOLE = pl.BlockSpec(memory_space=pltpu.VMEM)
UNROLL = 8
STEP = 8
LANES = 128


def column_row(cols_ref, owner, count):
    return cols_ref[:, pl.ds(pl.multiple_of(owner * count, LANES), count)]


def flip(cols, ny, nz):
    return lax.rem(ny - cols // nz, ny) * nz + lax.rem(nz - cols % nz, nz)


def one_hot(row, base, size):
    position = lax.broadcasted_iota(jnp.int32, (size, row.shape[1]), 0) + base
    return jnp.where(row == position, 1.0, 0.0).astype(BF16)


def dot_t(left_side, right_side):
    dims = (((1,), (1,)), ((), ()))
    return lax.dot_general(left_side, right_side, dims, preferred_element_type=F32)


def mirror_kernel(span, nz, me_ref, kernel_ref, cols_ref, out_ref, first_ref):
    nx, count = kernel_ref.shape
    row = lax.broadcasted_iota(jnp.int32, (nx, nx), 0)
    column = lax.broadcasted_iota(jnp.int32, (nx, nx), 1)
    swap = jnp.where(lax.rem(row + column, nx) == 0, 1.0, 0.0).astype(BF16)
    mirrored = dot(swap, kernel_ref[...].astype(BF16)).astype(BF16)
    out_ref[...] = mirrored
    local_cols = column_row(cols_ref, me_ref[0], count) - me_ref[0] * span
    target = jnp.where(local_cols < nz, lax.rem(nz - local_cols, nz), -1)
    first_ref[...] = dot_t(mirrored, one_hot(target, 0, nz)).astype(BF16)


def mirror(me, kernel, cols, span, nz):
    nx = kernel.shape[0]
    return pl.pallas_call(
        functools.partial(mirror_kernel, span, nz),
        out_shape=[jax.ShapeDtypeStruct(kernel.shape, BF16), jax.ShapeDtypeStruct((nx, nz), BF16)],
        in_specs=[SCALARS, WHOLE, WHOLE],
        out_specs=[WHOLE] * 2,
        cost_estimate=cost(2 * nx * nx * kernel.shape[1], 6 * kernel.size),
        name="mirror",
    )(me, kernel, cols)


def expand_kernel(scale, groups, span, ny, me_ref, own_ref, neg_ref, first_ref, cols_ref, out_ref, hot):
    nx, count = own_ref.shape
    length = out_ref.shape[2]
    wide = 2 * length
    me = me_ref[0]
    both = jnp.concatenate([own_ref[...].astype(BF16), neg_ref[...]], 1)
    mine = column_row(cols_ref, me, count) - me * span
    theirs = flip(column_row(cols_ref, groups - 1 - me, count), ny, length) - me * span
    group = jnp.concatenate([mine, theirs + span], 1) // wide
    group = group - jnp.concatenate(
        [jnp.zeros((1, count), jnp.int32), jnp.full((1, count), span // wide, jnp.int32)], 1
    )
    hot[:, :count] = one_hot(mine & (wide - 1), 0, wide)
    hot[:, count:] = one_hot(theirs & (wide - 1), 0, wide)

    def step(number, carry):
        sides = []
        for k in range(2):
            wanted = jnp.where(group == 2 * number + k, 1.0, 0.0).astype(BF16)
            sides.append(both * wanted)
        total = dot_t(jnp.concatenate(sides, 0), hot[...])
        for k in range(2):
            for half in range(2):
                out_ref[4 * number + 2 * k + half] = (
                    total[k * nx : (k + 1) * nx, half * length : (half + 1) * length] * scale
                )
        return carry

    lax.fori_loop(0, out_ref.shape[0] // 4, step, 0)
    out_ref[0] = out_ref[0] + first_ref[...].astype(F32) * scale


def expand(me, kernel, neg, first, cols, groups, ny, length, scale):
    nx, count = kernel.shape
    rows = ny // groups
    return pl.pallas_call(
        functools.partial(expand_kernel, scale, groups, rows * length, ny),
        out_shape=jax.ShapeDtypeStruct((rows, nx, length), F32),
        in_specs=[SCALARS] + [WHOLE] * 4,
        out_specs=WHOLE,
        scratch_shapes=[pltpu.VMEM((2 * length, 2 * count), BF16)],
        cost_estimate=cost(4 * nx * count * rows * length, 4 * nx * (count + rows * length)),
        name="expand",
    )(me, kernel, neg, first, cols)


PAD = 1


def unload(hold, first, out_ref):
    lines, _, count, _ = out_ref.shape

    def step(line, carry):
        for c in range(2):
            out_ref[line, c] = hold[c, pl.ds((first + line) * (count + PAD), count), :].astype(BF16)
        return carry

    lax.fori_loop(0, lines, step, 0, unroll=min(8, lines))


def forward_kernel(parts, base, cuts, me_ref, grid_ref, own_ref, *refs):
    piece_refs = refs[:parts]
    if parts > 1:
        zt_ref, yt_ref, their_ref = refs[parts : parts + 3]
        per = piece_refs[0].shape[0]
        for slot, piece_ref in enumerate(piece_refs):
            their_ref[pl.ds((me_ref[0] ^ slot) * per, per)] = piece_ref[...]
    else:
        their_ref, zt_ref, yt_ref = refs[:3]
    out_refs, hold = refs[3 + parts - (parts == 1) : -1], refs[-1]
    count, ny, nz = own_ref.shape[1:]
    tiles = ny // their_ref.shape[1]
    zt, yt = zt_ref[...], yt_ref[...]

    def step(pair, carry):
        lines = []
        for k in range(2):
            x = 2 * pair + k
            theirs = their_ref[pl.ds((base + x) * tiles, tiles)].reshape(ny, nz)
            lines.append(jnp.concatenate([own_ref[0, x] * theirs, own_ref[1, x] * theirs], 1))
        first = dot(jnp.concatenate(lines, 0), zt).astype(BF16)
        stack = jnp.concatenate(
            [
                jnp.concatenate([first[:ny, :nz], first[ny:, :nz]], 1),
                jnp.concatenate([first[:ny, nz:], first[ny:, nz:]], 1),
            ],
            0,
        )
        second = dot(yt, stack)
        for k in range(2):
            for c in range(2):
                hold[c, pl.ds(2 * pair + k, ny, stride=count + PAD), :] = second[
                    c * ny : (c + 1) * ny, k * nz : (k + 1) * nz
                ]
        return carry

    lax.fori_loop(0, count // 2, step, 0, unroll=min(UNROLL, count // 2))
    part = ny // len(out_refs)
    for number, out_ref in enumerate(out_refs):
        owner = grid_ref[0] ^ (number // cuts)
        unload(hold, (owner * cuts + number % cuts) * part, out_ref)


def forward(me, grid_pos, own, pieces, half, count, zt, yt, groups, cuts):
    ny, nz = own.shape[2:]
    part = ny // (groups * cuts)
    parts = len(pieces)
    shape = jax.ShapeDtypeStruct((part, 2, count, nz), BF16)
    their = jax.ShapeDtypeStruct((parts * pieces[0].shape[0],) + pieces[0].shape[1:], BF16)
    outs = ([their] if parts > 1 else []) + [shape] * (groups * cuts)
    return pl.pallas_call(
        functools.partial(forward_kernel, parts, half * count, cuts),
        grid=(1,),
        out_shape=outs,
        in_specs=[SCALARS, SCALARS, spec((2, count, ny, nz), lambda i: (0, half, 0, 0))]
        + [spec(p.shape) for p in pieces]
        + [spec(zt.shape), spec(yt.shape)],
        out_specs=[spec(o.shape) for o in outs],
        scratch_shapes=[pltpu.VMEM((2, ny * (count + PAD), nz), F32)],
        cost_estimate=cost(2 * count * ny * nz * 2 * (2 * ny + 2 * nz), 12 * count * ny * nz),
        name="forward",
    )(me, grid_pos, own, *pieces, zt, yt)


def middle_kernel(groups, halves, grid_ref, *refs):
    in_refs = refs[:groups]
    kern_ref, xt_ref, ixt_ref = refs[groups : groups + 3]
    out_refs, hold = refs[groups + 3 : -1], refs[-1]
    count, nx, nz = kern_ref.shape
    xt, ixt = xt_ref[...], ixt_ref[...]

    def step(pair, carry):
        lines, factors = [], []
        for k in range(2):
            line = 2 * pair + k
            lines.append(jnp.concatenate([r[line, c] for c in range(2) for r in in_refs], 0))
            factors.append(kern_ref[line])
        factor = jnp.concatenate(factors, 1)
        spectrum = dot(xt, jnp.concatenate(lines, 1))
        scaled = jnp.concatenate(
            [(spectrum[:nx] * factor).astype(BF16), (spectrum[nx:] * factor).astype(BF16)], 0
        )
        third = dot(ixt, scaled)
        for k in range(2):
            for c in range(2):
                hold[c, pl.ds(2 * pair + k, nx, stride=count + PAD), :] = third[
                    c * nx : (c + 1) * nx, k * nz : (k + 1) * nz
                ]
        return carry

    lax.fori_loop(0, count // 2, step, 0, unroll=min(UNROLL, count // 2))
    rows = nx // (groups * halves)
    for number, out_ref in enumerate(out_refs):
        owner = grid_ref[0] ^ (number // halves)
        unload(hold, (owner * halves + number % halves) * rows, out_ref)


def middle(grid_pos, pieces, kern, cut, xt, ixt, halves):
    groups = len(pieces)
    count, nx, nz = pieces[0].shape[0], kern.shape[1], kern.shape[2]
    rows = nx // (groups * halves)
    shape = jax.ShapeDtypeStruct((rows, 2, count, nz), BF16)
    return pl.pallas_call(
        functools.partial(middle_kernel, groups, halves),
        grid=(1,),
        out_shape=[shape] * (groups * halves),
        in_specs=[SCALARS]
        + [spec(p.shape) for p in pieces]
        + [spec((count, nx, nz), lambda i: (cut, 0, 0)), spec(xt.shape), spec(ixt.shape)],
        out_specs=[spec(shape.shape)] * (groups * halves),
        scratch_shapes=[pltpu.VMEM((2, nx * (count + PAD), nz), F32)],
        cost_estimate=cost(16 * nx * nx * count * nz, 12 * count * nx * nz),
        name="middle",
    )(grid_pos, *pieces, kern, xt, ixt)


def backward_kernel(number, has_total, *refs):
    in_refs = refs[:number]
    their_ref, weight_ref, yt_ref, zt_ref = refs[number : number + 4]
    total_ref = refs[number + 4] if has_total == 2 else None
    out_ref = refs[-1]
    count, ny, nz = out_ref.shape[1:]
    tiles = ny // their_ref.shape[1]
    zt, yt = zt_ref[...], yt_ref[...]
    weight = weight_ref[0]

    def step(pair, carry):
        lines = []
        for k in range(2):
            x = 2 * pair + k
            lines.append(jnp.concatenate([r[x, c] for c in range(2) for r in in_refs], 0))
        fourth = dot(yt, jnp.concatenate(lines, 1)).astype(BF16)
        stack = jnp.concatenate(
            [
                jnp.concatenate([fourth[:ny, k * nz : (k + 1) * nz], fourth[ny:, k * nz : (k + 1) * nz]], 1)
                for k in range(2)
            ],
            0,
        )
        potential = dot(stack, zt)
        for k in range(2):
            x = 2 * pair + k
            theirs = their_ref[pl.ds(x * tiles, tiles)].reshape(ny, nz).astype(F32) * weight
            for n in range(2):
                term = potential[k * ny : (k + 1) * ny, n * nz : (n + 1) * nz] * theirs
                if total_ref is None:
                    out_ref[n, x] = -term
                else:
                    out_ref[n, x] = total_ref[n, x] - term
        return carry

    lax.fori_loop(0, count // 2, step, 0, unroll=min(UNROLL, count // 2))


def backward(pieces, bases, their, weight, yt, zt, total, accumulate, part_number, count, slab):
    ny, nz = sum(p.shape[2] for p in pieces), pieces[0].shape[3]
    number = len(pieces)
    step = min(STEP, count)
    steps = count // step
    begin = part_number * steps
    tiles = ny // their.shape[1]
    block = spec((2, step, ny, nz), lambda i: (0, begin + i, 0, 0))
    has_total = 0 if total is None else (2 if accumulate else 1)
    extra = [] if total is None else [total]
    extra_specs = [] if total is None else [block if accumulate else pl.BlockSpec(memory_space=pl.ANY)]

    def rows_of(piece, base):
        return spec((step,) + piece.shape[1:], lambda i: (base // step + i, 0, 0, 0))

    return pl.pallas_call(
        functools.partial(backward_kernel, number, has_total),
        grid=(steps,),
        out_shape=jax.ShapeDtypeStruct((2, slab, ny, nz), F32),
        in_specs=[rows_of(p, b) for p, b in zip(pieces, bases)]
        + [spec((step * tiles,) + their.shape[1:], lambda i: (begin + i, 0, 0))]
        + [SCALARS, spec(yt.shape), spec(zt.shape)]
        + extra_specs,
        out_specs=block,
        input_output_aliases={number + 4: 0} if extra else {},
        cost_estimate=cost(2 * count * ny * nz * 2 * (2 * ny + 2 * nz), 24 * count * ny * nz),
        name="backward",
    )(*pieces, their, weight, yt, zt, *extra)


TILE = 16


def after(value, *others):
    return lax.optimization_barrier((value, others))[0]


def shift(value, axis, size, mask):
    return lax.ppermute(value, axis, [(i, i ^ mask) for i in range(size)]) if mask else value


def split_kernel(me_ref, in_ref, *out_refs):
    per = out_refs[0].shape[0]
    for slot, out_ref in enumerate(out_refs):
        out_ref[...] = in_ref[0, pl.ds((me_ref[0] ^ slot) * per, per)]


def split(me, value, band, chunk, tiles, parts):
    shape = jax.ShapeDtypeStruct((tiles // parts,) + value.shape[2:], value.dtype)
    return pl.pallas_call(
        split_kernel,
        grid=(1,),
        out_shape=[shape] * parts,
        in_specs=[SCALARS, spec((1, tiles) + value.shape[2:], lambda i: (band, chunk, 0, 0))],
        out_specs=[spec(shape.shape)] * parts,
        cost_estimate=cost(0, 4 * tiles * TILE * value.shape[3]),
        name="split",
    )(me, value)


def pick_kernel(parts, choice_ref, *refs):
    in_refs, out_refs, hold = refs[:parts], refs[parts:-1], refs[-1]
    for slot, in_ref in enumerate(in_refs):
        hold[slot] = in_ref[...]
    for slot, out_ref in enumerate(out_refs):
        out_ref[...] = hold[choice_ref[slot]]


def pick(choice, pieces):
    parts, shape = len(pieces), pieces[0].shape
    return pl.pallas_call(
        functools.partial(pick_kernel, parts),
        out_shape=[jax.ShapeDtypeStruct(shape, pieces[0].dtype)] * parts,
        in_specs=[SCALARS] + [WHOLE] * parts,
        out_specs=[WHOLE] * parts,
        scratch_shapes=[pltpu.VMEM((parts,) + shape, pieces[0].dtype)],
        cost_estimate=cost(0, 4 * parts * math.prod(shape)),
        name="pick",
    )(choice, *pieces)


def pick_stacked_kernel(parts, choice_ref, *refs):
    in_refs, out_ref, hold = refs[:parts], refs[-2], refs[-1]
    for slot, in_ref in enumerate(in_refs):
        hold[slot] = in_ref[...]
    for number in range(parts):
        out_ref[number] = hold[choice_ref[number]]


def pick_stacked(choice, pieces):
    parts, shape = len(pieces), pieces[0].shape
    return pl.pallas_call(
        functools.partial(pick_stacked_kernel, parts),
        out_shape=jax.ShapeDtypeStruct((parts,) + shape, pieces[0].dtype),
        in_specs=[SCALARS] + [WHOLE] * parts,
        out_specs=WHOLE,
        scratch_shapes=[pltpu.VMEM((parts,) + shape, pieces[0].dtype)],
        cost_estimate=cost(0, 4 * parts * math.prod(shape)),
        name="pick",
    )(choice, *pieces)


def local(orbitals, occupation, partner, col_index, kernel):
    bands, groups = lax.axis_size("band"), lax.axis_size("grid")
    slab, ny, nz = orbitals.shape[1:]
    nx, _ = kernel.shape
    lines = ny // groups
    band_pos, me = lax.axis_index("band"), lax.axis_index("grid")
    band_slots = jnp.arange(bands, dtype=jnp.int32)
    my_band = band_pos.astype(jnp.int32).reshape(1)
    choice = jnp.take(partner, band_slots ^ band_pos) ^ band_pos
    pick_choice = partner ^ band_pos
    tiled = orbitals.reshape(2, slab * ny // TILE, TILE, nz)

    def swap(value, slot):
        return shift(value, "grid", groups, slot)

    def exchange(value):
        return lax.all_to_all(value, "band", split_axis=0, concat_axis=0, tiled=True)

    def slotwise(sent):
        return [shift(piece, "band", bands, slot) for slot, piece in enumerate(sent)]

    my_grid = me.astype(jnp.int32).reshape(1)
    cols = col_index.reshape(1, -1)
    blocks = tiled[0].reshape(bands, -1, TILE, nz)
    sent = [
        lax.dynamic_index_in_dim(blocks, band_pos ^ slot, 0, keepdims=False) for slot in range(bands)
    ]
    arrived = slotwise(sent)
    sent1 = split(my_band, after(tiled, *sent), 1, 0, slab * ny // TILE, bands)

    mirror_of = [(i, groups - 1 - i) for i in range(groups)]
    mirror_first = [(i, (groups - i) % groups) for i in range(groups)]
    mirrored, first_line = mirror(my_grid, after(kernel, *sent), cols, lines * nz, nz)
    neg = lax.ppermute(mirrored, "grid", mirror_of)
    first = lax.ppermute(first_line, "grid", mirror_first)

    def slots(table, axis):
        shape = table.shape
        blocks = table.reshape(shape[:axis] + (2, groups, shape[axis] // (2 * groups)) + shape[axis + 1 :])
        order = jnp.arange(groups, dtype=jnp.int32) ^ me
        return jnp.take(blocks, order, axis=axis + 1).reshape(shape)

    xleft, xright = block_tables(nx)
    yleft, yright = block_tables(ny)
    zleft, zright = block_tables(nz)
    x_forward, y_inverse = slots(xleft, 1), slots(yright, 1)
    cuts = 2 if lines % 32 == 0 else 1
    parts = 2 if slab % 32 == 0 else 1

    picked = pick(choice, after(arrived, mirrored, first_line, *sent1))
    fetched = slotwise(picked)
    kern = expand(
        my_grid, after(kernel, *picked), neg, first, cols, groups, ny, nz, 0.5 / (nx * ny * nz)
    )
    arrived = slotwise(after(sent1, kern))

    def outward(pieces):
        outs = forward(my_band, my_grid, orbitals, pieces, 0, slab, zright, yleft, groups, cuts)
        their, sent = (outs[0], outs[1:]) if len(pieces) > 1 else (pieces[0], outs)
        moved = [
            [swap(sent[slot * cuts + cut], slot) for slot in range(groups)]
            for cut in range(cuts)
        ]
        return their, sent, moved

    their0, sent, moved0 = outward(fetched)
    picked = pick_stacked(pick_choice, after(arrived, *sent))
    their1 = exchange(picked.reshape(tiled.shape[1:]))

    def centre(cut, moved, halves):
        return middle(my_grid, moved[cut], kern, cut, x_forward, xright, halves)

    def home(values):
        return [swap(value, slot) for slot, value in enumerate(values)]

    def ending(m, total, back, bases, h, count, their):
        weight = lax.dynamic_slice_in_dim(occupation, partner[band_pos] * 2 + m, 1, 0)
        pieces = [piece for by_cut in zip(*back) for piece in by_cut]
        return backward(
            pieces, bases * groups, their, weight, y_inverse, zleft, total, m > 0, h, count, slab
        )

    answers = [centre(cut, moved0, 1) for cut in range(cuts)]
    back0 = [home(answers[cut]) for cut in range(cuts)]
    their1, _, moved1 = outward([after(their1, *answers[-1])])

    last = cuts - 1
    answers = [centre(cut, moved1, parts if cut == last else 1) for cut in range(cuts)]
    early = [home(answers[cut]) for cut in range(last)]
    rows = slab // parts
    late = [answers[last][h::parts] for h in range(parts)]
    late[0] = home(late[0])
    total = None
    for h in range(parts):
        if h == parts - 1:
            back0[0] = after(back0[0], *answers[last])
        total = ending(0, total, back0, (h * rows,) * cuts, h, rows, their0)
    for h in range(1, parts):
        late[h] = home(after(late[h], total))
    for h in range(parts):
        bases = (h * rows,) * last + (0,)
        total = ending(1, total, early + [late[h]], bases, h, rows, their1)
    return total


def solution(mesh):
    in_specs = (P("band", "grid", None, None), P(), P(), P(), P(None, "grid"))
    out_specs = P("band", "grid", None, None)
    return jax.shard_map(local, mesh=mesh, in_specs=in_specs, out_specs=out_specs, check_vma=False)
```

```python
import functools
import math

import jax
import jax.numpy as jnp
from jax import lax
from jax.experimental import pallas as pl
from jax.experimental.pallas import tpu as pltpu
from jax.sharding import PartitionSpec as P


BF16 = jnp.bfloat16
F32 = jnp.float32


def tables(length):
    counter = jnp.arange(length, dtype=jnp.int32)
    product = counter[:, None] * counter[None, :] % length
    angles = product.astype(F32) * (2.0 * math.pi / length)
    return jnp.cos(angles).astype(BF16), jnp.sin(angles).astype(BF16)


def block_tables(length):
    cosine, sine = tables(length)
    left = jnp.concatenate(
        [jnp.concatenate([cosine, sine], 1), jnp.concatenate([-sine, cosine], 1)], 0
    )
    right = jnp.concatenate(
        [jnp.concatenate([cosine, -sine], 1), jnp.concatenate([sine, cosine], 1)], 0
    )
    return left, right


def dot(left_side, right_side):
    return jnp.dot(left_side, right_side, preferred_element_type=F32)


def cost(flops, moved):
    return pl.CostEstimate(flops=int(flops), bytes_accessed=int(moved), transcendentals=0)


def spec(shape, index=None):
    rank = len(shape)
    return pl.BlockSpec(shape, index or (lambda *_: (0,) * rank))


SCALARS = pl.BlockSpec(memory_space=pltpu.SMEM)
WHOLE = pl.BlockSpec(memory_space=pltpu.VMEM)
UNROLL = 8
STEP = 8
LANES = 128


def column_row(cols_ref, owner, count):
    return cols_ref[:, pl.ds(pl.multiple_of(owner * count, LANES), count)]


def flip(cols, ny, nz):
    return lax.rem(ny - cols // nz, ny) * nz + lax.rem(nz - cols % nz, nz)


def one_hot(row, base, size):
    position = lax.broadcasted_iota(jnp.int32, (size, row.shape[1]), 0) + base
    return jnp.where(row == position, 1.0, 0.0).astype(BF16)


def dot_t(left_side, right_side):
    dims = (((1,), (1,)), ((), ()))
    return lax.dot_general(left_side, right_side, dims, preferred_element_type=F32)


def mirror_kernel(span, nz, me_ref, kernel_ref, cols_ref, out_ref, first_ref):
    nx, count = kernel_ref.shape
    row = lax.broadcasted_iota(jnp.int32, (nx, nx), 0)
    column = lax.broadcasted_iota(jnp.int32, (nx, nx), 1)
    swap = jnp.where(lax.rem(row + column, nx) == 0, 1.0, 0.0).astype(BF16)
    mirrored = dot(swap, kernel_ref[...].astype(BF16)).astype(BF16)
    out_ref[...] = mirrored
    local_cols = column_row(cols_ref, me_ref[0], count) - me_ref[0] * span
    target = jnp.where(local_cols < nz, lax.rem(nz - local_cols, nz), -1)
    first_ref[...] = dot_t(mirrored, one_hot(target, 0, nz)).astype(BF16)


def mirror(me, kernel, cols, span, nz):
    nx = kernel.shape[0]
    return pl.pallas_call(
        functools.partial(mirror_kernel, span, nz),
        out_shape=[jax.ShapeDtypeStruct(kernel.shape, BF16), jax.ShapeDtypeStruct((nx, nz), BF16)],
        in_specs=[SCALARS, WHOLE, WHOLE],
        out_specs=[WHOLE] * 2,
        cost_estimate=cost(2 * nx * nx * kernel.shape[1], 6 * kernel.size),
        name="mirror",
    )(me, kernel, cols)


def expand_kernel(scale, groups, span, ny, me_ref, own_ref, neg_ref, first_ref, cols_ref, out_ref, hot):
    nx, count = own_ref.shape
    length = out_ref.shape[2]
    wide = 2 * length
    me = me_ref[0]
    both = jnp.concatenate([own_ref[...].astype(BF16), neg_ref[...]], 1)
    mine = column_row(cols_ref, me, count) - me * span
    theirs = flip(column_row(cols_ref, groups - 1 - me, count), ny, length) - me * span
    group = jnp.concatenate([mine, theirs + span], 1) // wide
    group = group - jnp.concatenate(
        [jnp.zeros((1, count), jnp.int32), jnp.full((1, count), span // wide, jnp.int32)], 1
    )
    hot[:, :count] = one_hot(mine & (wide - 1), 0, wide)
    hot[:, count:] = one_hot(theirs & (wide - 1), 0, wide)

    def step(number, carry):
        sides = []
        for k in range(2):
            wanted = jnp.where(group == 2 * number + k, 1.0, 0.0).astype(BF16)
            sides.append(both * wanted)
        total = dot_t(jnp.concatenate(sides, 0), hot[...])
        for k in range(2):
            for half in range(2):
                out_ref[4 * number + 2 * k + half] = (
                    total[k * nx : (k + 1) * nx, half * length : (half + 1) * length] * scale
                )
        return carry

    lax.fori_loop(0, out_ref.shape[0] // 4, step, 0)
    out_ref[0] = out_ref[0] + first_ref[...].astype(F32) * scale


def expand(me, kernel, neg, first, cols, groups, ny, length, scale):
    nx, count = kernel.shape
    rows = ny // groups
    return pl.pallas_call(
        functools.partial(expand_kernel, scale, groups, rows * length, ny),
        out_shape=jax.ShapeDtypeStruct((rows, nx, length), F32),
        in_specs=[SCALARS] + [WHOLE] * 4,
        out_specs=WHOLE,
        scratch_shapes=[pltpu.VMEM((2 * length, 2 * count), BF16)],
        cost_estimate=cost(4 * nx * count * rows * length, 4 * nx * (count + rows * length)),
        name="expand",
    )(me, kernel, neg, first, cols)


PAD = 1


def unload(hold, first, out_ref):
    lines, _, count, _ = out_ref.shape

    def step(line, carry):
        for c in range(2):
            out_ref[line, c] = hold[c, pl.ds((first + line) * (count + PAD), count), :].astype(BF16)
        return carry

    lax.fori_loop(0, lines, step, 0, unroll=min(8, lines))


def forward_kernel(parts, base, cuts, me_ref, grid_ref, own_ref, *refs):
    piece_refs = refs[:parts]
    if parts > 1:
        zt_ref, yt_ref, their_ref = refs[parts : parts + 3]
        per = piece_refs[0].shape[0]
        for slot, piece_ref in enumerate(piece_refs):
            their_ref[pl.ds((me_ref[0] ^ slot) * per, per)] = piece_ref[...]
    else:
        their_ref, zt_ref, yt_ref = refs[:3]
    out_refs, hold = refs[3 + parts - (parts == 1) : -1], refs[-1]
    count, ny, nz = own_ref.shape[1:]
    tiles = ny // their_ref.shape[1]
    zt, yt = zt_ref[...], yt_ref[...]

    def step(pair, carry):
        lines = []
        for k in range(2):
            x = 2 * pair + k
            theirs = their_ref[pl.ds((base + x) * tiles, tiles)].reshape(ny, nz)
            lines.append(jnp.concatenate([own_ref[0, x] * theirs, own_ref[1, x] * theirs], 1))
        first = dot(jnp.concatenate(lines, 0), zt).astype(BF16)
        stack = jnp.concatenate(
            [
                jnp.concatenate([first[:ny, :nz], first[ny:, :nz]], 1),
                jnp.concatenate([first[:ny, nz:], first[ny:, nz:]], 1),
            ],
            0,
        )
        second = dot(yt, stack)
        for k in range(2):
            for c in range(2):
                hold[c, pl.ds(2 * pair + k, ny, stride=count + PAD), :] = second[
                    c * ny : (c + 1) * ny, k * nz : (k + 1) * nz
                ]
        return carry

    lax.fori_loop(0, count // 2, step, 0, unroll=min(UNROLL, count // 2))
    part = ny // len(out_refs)
    for number, out_ref in enumerate(out_refs):
        owner = grid_ref[0] ^ (number // cuts)
        unload(hold, (owner * cuts + number % cuts) * part, out_ref)


def forward(me, grid_pos, own, pieces, half, count, zt, yt, groups, cuts):
    ny, nz = own.shape[2:]
    part = ny // (groups * cuts)
    parts = len(pieces)
    shape = jax.ShapeDtypeStruct((part, 2, count, nz), BF16)
    their = jax.ShapeDtypeStruct((parts * pieces[0].shape[0],) + pieces[0].shape[1:], BF16)
    outs = ([their] if parts > 1 else []) + [shape] * (groups * cuts)
    return pl.pallas_call(
        functools.partial(forward_kernel, parts, half * count, cuts),
        grid=(1,),
        out_shape=outs,
        in_specs=[SCALARS, SCALARS, spec((2, count, ny, nz), lambda i: (0, half, 0, 0))]
        + [spec(p.shape) for p in pieces]
        + [spec(zt.shape), spec(yt.shape)],
        out_specs=[spec(o.shape) for o in outs],
        scratch_shapes=[pltpu.VMEM((2, ny * (count + PAD), nz), F32)],
        cost_estimate=cost(2 * count * ny * nz * 2 * (2 * ny + 2 * nz), 12 * count * ny * nz),
        name="forward",
    )(me, grid_pos, own, *pieces, zt, yt)


def middle_kernel(groups, halves, grid_ref, *refs):
    in_refs = refs[:groups]
    kern_ref, xt_ref, ixt_ref = refs[groups : groups + 3]
    out_refs, hold = refs[groups + 3 : -1], refs[-1]
    count, nx, nz = kern_ref.shape
    xt, ixt = xt_ref[...], ixt_ref[...]

    def step(pair, carry):
        lines, factors = [], []
        for k in range(2):
            line = 2 * pair + k
            lines.append(jnp.concatenate([r[line, c] for c in range(2) for r in in_refs], 0))
            factors.append(kern_ref[line])
        factor = jnp.concatenate(factors, 1)
        spectrum = dot(xt, jnp.concatenate(lines, 1))
        scaled = jnp.concatenate(
            [(spectrum[:nx] * factor).astype(BF16), (spectrum[nx:] * factor).astype(BF16)], 0
        )
        third = dot(ixt, scaled)
        for k in range(2):
            for c in range(2):
                hold[c, pl.ds(2 * pair + k, nx, stride=count + PAD), :] = third[
                    c * nx : (c + 1) * nx, k * nz : (k + 1) * nz
                ]
        return carry

    lax.fori_loop(0, count // 2, step, 0, unroll=min(UNROLL, count // 2))
    rows = nx // (groups * halves)
    for number, out_ref in enumerate(out_refs):
        owner = grid_ref[0] ^ (number // halves)
        unload(hold, (owner * halves + number % halves) * rows, out_ref)


def middle(grid_pos, pieces, kern, cut, xt, ixt, halves):
    groups = len(pieces)
    count, nx, nz = pieces[0].shape[0], kern.shape[1], kern.shape[2]
    rows = nx // (groups * halves)
    shape = jax.ShapeDtypeStruct((rows, 2, count, nz), BF16)
    return pl.pallas_call(
        functools.partial(middle_kernel, groups, halves),
        grid=(1,),
        out_shape=[shape] * (groups * halves),
        in_specs=[SCALARS]
        + [spec(p.shape) for p in pieces]
        + [spec((count, nx, nz), lambda i: (cut, 0, 0)), spec(xt.shape), spec(ixt.shape)],
        out_specs=[spec(shape.shape)] * (groups * halves),
        scratch_shapes=[pltpu.VMEM((2, nx * (count + PAD), nz), F32)],
        cost_estimate=cost(16 * nx * nx * count * nz, 12 * count * nx * nz),
        name="middle",
    )(grid_pos, *pieces, kern, xt, ixt)


def backward_kernel(number, has_total, *refs):
    in_refs = refs[:number]
    their_ref, weight_ref, yt_ref, zt_ref = refs[number : number + 4]
    total_ref = refs[number + 4] if has_total == 2 else None
    out_ref = refs[-1]
    count, ny, nz = out_ref.shape[1:]
    tiles = ny // their_ref.shape[1]
    zt, yt = zt_ref[...], yt_ref[...]
    weight = weight_ref[0]

    def step(pair, carry):
        lines = []
        for k in range(2):
            x = 2 * pair + k
            lines.append(jnp.concatenate([r[x, c] for c in range(2) for r in in_refs], 0))
        fourth = dot(yt, jnp.concatenate(lines, 1)).astype(BF16)
        stack = jnp.concatenate(
            [
                jnp.concatenate([fourth[:ny, k * nz : (k + 1) * nz], fourth[ny:, k * nz : (k + 1) * nz]], 1)
                for k in range(2)
            ],
            0,
        )
        potential = dot(stack, zt)
        for k in range(2):
            x = 2 * pair + k
            theirs = their_ref[pl.ds(x * tiles, tiles)].reshape(ny, nz).astype(F32) * weight
            for n in range(2):
                term = potential[k * ny : (k + 1) * ny, n * nz : (n + 1) * nz] * theirs
                if total_ref is None:
                    out_ref[n, x] = -term
                else:
                    out_ref[n, x] = total_ref[n, x] - term
        return carry

    lax.fori_loop(0, count // 2, step, 0, unroll=min(UNROLL, count // 2))


def backward(pieces, bases, their, weight, yt, zt, total, accumulate, part_number, count, slab):
    ny, nz = sum(p.shape[2] for p in pieces), pieces[0].shape[3]
    number = len(pieces)
    step = min(STEP, count)
    steps = count // step
    begin = part_number * steps
    tiles = ny // their.shape[1]
    block = spec((2, step, ny, nz), lambda i: (0, begin + i, 0, 0))
    has_total = 0 if total is None else (2 if accumulate else 1)
    extra = [] if total is None else [total]
    extra_specs = [] if total is None else [block if accumulate else pl.BlockSpec(memory_space=pl.ANY)]

    def rows_of(piece, base):
        return spec((step,) + piece.shape[1:], lambda i: (base // step + i, 0, 0, 0))

    return pl.pallas_call(
        functools.partial(backward_kernel, number, has_total),
        grid=(steps,),
        out_shape=jax.ShapeDtypeStruct((2, slab, ny, nz), F32),
        in_specs=[rows_of(p, b) for p, b in zip(pieces, bases)]
        + [spec((step * tiles,) + their.shape[1:], lambda i: (begin + i, 0, 0))]
        + [SCALARS, spec(yt.shape), spec(zt.shape)]
        + extra_specs,
        out_specs=block,
        input_output_aliases={number + 4: 0} if extra else {},
        cost_estimate=cost(2 * count * ny * nz * 2 * (2 * ny + 2 * nz), 24 * count * ny * nz),
        name="backward",
    )(*pieces, their, weight, yt, zt, *extra)


TILE = 16


def after(value, *others):
    return lax.optimization_barrier((value, others))[0]


def shift(value, axis, size, mask):
    return lax.ppermute(value, axis, [(i, i ^ mask) for i in range(size)]) if mask else value


def split_kernel(me_ref, in_ref, *out_refs):
    per = out_refs[0].shape[0]
    for slot, out_ref in enumerate(out_refs):
        out_ref[...] = in_ref[0, pl.ds((me_ref[0] ^ slot) * per, per)]


def split(me, value, band, chunk, tiles, parts):
    shape = jax.ShapeDtypeStruct((tiles // parts,) + value.shape[2:], value.dtype)
    return pl.pallas_call(
        split_kernel,
        grid=(1,),
        out_shape=[shape] * parts,
        in_specs=[SCALARS, spec((1, tiles) + value.shape[2:], lambda i: (band, chunk, 0, 0))],
        out_specs=[spec(shape.shape)] * parts,
        cost_estimate=cost(0, 4 * tiles * TILE * value.shape[3]),
        name="split",
    )(me, value)


def pick_kernel(parts, choice_ref, *refs):
    in_refs, out_refs, hold = refs[:parts], refs[parts:-1], refs[-1]
    for slot, in_ref in enumerate(in_refs):
        hold[slot] = in_ref[...]
    for slot, out_ref in enumerate(out_refs):
        out_ref[...] = hold[choice_ref[slot]]


def pick(choice, pieces):
    parts, shape = len(pieces), pieces[0].shape
    return pl.pallas_call(
        functools.partial(pick_kernel, parts),
        out_shape=[jax.ShapeDtypeStruct(shape, pieces[0].dtype)] * parts,
        in_specs=[SCALARS] + [WHOLE] * parts,
        out_specs=[WHOLE] * parts,
        scratch_shapes=[pltpu.VMEM((parts,) + shape, pieces[0].dtype)],
        cost_estimate=cost(0, 4 * parts * math.prod(shape)),
        name="pick",
    )(choice, *pieces)


def pick_stacked_kernel(parts, choice_ref, *refs):
    in_refs, out_ref, hold = refs[:parts], refs[-2], refs[-1]
    for slot, in_ref in enumerate(in_refs):
        hold[slot] = in_ref[...]
    for number in range(parts):
        out_ref[number] = hold[choice_ref[number]]


def pick_stacked(choice, pieces):
    parts, shape = len(pieces), pieces[0].shape
    return pl.pallas_call(
        functools.partial(pick_stacked_kernel, parts),
        out_shape=jax.ShapeDtypeStruct((parts,) + shape, pieces[0].dtype),
        in_specs=[SCALARS] + [WHOLE] * parts,
        out_specs=WHOLE,
        scratch_shapes=[pltpu.VMEM((parts,) + shape, pieces[0].dtype)],
        cost_estimate=cost(0, 4 * parts * math.prod(shape)),
        name="pick",
    )(choice, *pieces)


def local(orbitals, occupation, partner, col_index, kernel):
    bands, groups = lax.axis_size("band"), lax.axis_size("grid")
    slab, ny, nz = orbitals.shape[1:]
    nx, _ = kernel.shape
    lines = ny // groups
    band_pos, me = lax.axis_index("band"), lax.axis_index("grid")
    band_slots = jnp.arange(bands, dtype=jnp.int32)
    my_band = band_pos.astype(jnp.int32).reshape(1)
    choice = jnp.take(partner, band_slots ^ band_pos) ^ band_pos
    pick_choice = partner ^ band_pos
    tiled = orbitals.reshape(2, slab * ny // TILE, TILE, nz)

    def swap(value, slot):
        return shift(value, "grid", groups, slot)

    def exchange(value):
        return lax.all_to_all(value, "band", split_axis=0, concat_axis=0, tiled=True)

    def slotwise(sent):
        moved = []
        for slot, piece in enumerate(sent):
            moved.append(shift(piece, "band", bands, slot))
        return moved

    my_grid = me.astype(jnp.int32).reshape(1)
    cols = col_index.reshape(1, -1)
    blocks = tiled[0].reshape(bands, -1, TILE, nz)
    sent = [
        lax.dynamic_index_in_dim(blocks, band_pos ^ slot, 0, keepdims=False) for slot in range(bands)
    ]
    arrived = slotwise(sent)
    sent1 = split(my_band, after(tiled, *sent), 1, 0, slab * ny // TILE, bands)

    mirror_of = [(i, groups - 1 - i) for i in range(groups)]
    mirror_first = [(i, (groups - i) % groups) for i in range(groups)]
    mirrored, first_line = mirror(my_grid, after(kernel, *sent), cols, lines * nz, nz)
    neg = lax.ppermute(mirrored, "grid", mirror_of)
    first = lax.ppermute(first_line, "grid", mirror_first)

    def slots(table, axis):
        shape = table.shape
        blocks = table.reshape(shape[:axis] + (2, groups, shape[axis] // (2 * groups)) + shape[axis + 1 :])
        order = jnp.arange(groups, dtype=jnp.int32) ^ me
        return jnp.take(blocks, order, axis=axis + 1).reshape(shape)

    xleft, xright = block_tables(nx)
    yleft, yright = block_tables(ny)
    zleft, zright = block_tables(nz)
    x_forward, y_inverse = slots(xleft, 1), slots(yright, 1)
    cuts = 2 if lines % 32 == 0 else 1
    parts = 2 if slab % 32 == 0 else 1

    picked = pick(choice, after(arrived, mirrored, first_line, *sent1))
    fetched = slotwise(picked)
    kern = expand(
        my_grid, after(kernel, *picked), neg, first, cols, groups, ny, nz, 0.5 / (nx * ny * nz)
    )
    arrived = slotwise(after(sent1, kern))

    def outward(pieces):
        outs = forward(my_band, my_grid, orbitals, pieces, 0, slab, zright, yleft, groups, cuts)
        their, sent = (outs[0], outs[1:]) if len(pieces) > 1 else (pieces[0], outs)
        moved = [
            [swap(sent[slot * cuts + cut], slot) for slot in range(groups)]
            for cut in range(cuts)
        ]
        return their, sent, moved

    their0, sent, moved0 = outward(fetched)
    picked = pick_stacked(pick_choice, after(arrived, *sent))
    their1 = exchange(picked.reshape(tiled.shape[1:]))

    def centre(cut, moved, halves):
        return middle(my_grid, moved[cut], kern, cut, x_forward, xright, halves)

    def home(values):
        return [swap(value, slot) for slot, value in enumerate(values)]

    def ending(m, total, back, bases, h, count, their):
        weight = lax.dynamic_slice_in_dim(occupation, partner[band_pos] * 2 + m, 1, 0)
        pieces = [piece for by_cut in zip(*back) for piece in by_cut]
        return backward(
            pieces, bases * groups, their, weight, y_inverse, zleft, total, m > 0, h, count, slab
        )

    answers = [centre(cut, moved0, 1) for cut in range(cuts)]
    back0 = [home(answers[cut]) for cut in range(cuts)]
    their1, _, moved1 = outward([after(their1, *answers[-1])])

    last = cuts - 1
    answers = [centre(cut, moved1, parts if cut == last else 1) for cut in range(cuts)]
    early = [home(answers[cut]) for cut in range(last)]
    rows = slab // parts
    late = [answers[last][h::parts] for h in range(parts)]
    late[0] = home(late[0])
    total = None
    for h in range(parts):
        if h == parts - 1:
            back0[0] = after(back0[0], *answers[last])
        total = ending(0, total, back0, (h * rows,) * cuts, h, rows, their0)
    for h in range(1, parts):
        late[h] = home(after(late[h], total))
    for h in range(parts):
        bases = (h * rows,) * last + (0,)
        total = ending(1, total, early + [late[h]], bases, h, rows, their1)
    return total


def solution(mesh):
    in_specs = (P("band", "grid", None, None), P(), P(), P(), P(None, "grid"))
    out_specs = P("band", "grid", None, None)
    return jax.shard_map(local, mesh=mesh, in_specs=in_specs, out_specs=out_specs, check_vma=False)
```

```python
import functools
import math

import jax
import jax.numpy as jnp
from jax import lax
from jax.experimental import pallas as pl
from jax.experimental.pallas import tpu as pltpu
from jax.sharding import PartitionSpec as P


BF16 = jnp.bfloat16
F32 = jnp.float32


def tables(length):
    counter = jnp.arange(length, dtype=jnp.int32)
    product = counter[:, None] * counter[None, :] % length
    angles = product.astype(F32) * (2.0 * math.pi / length)
    return jnp.cos(angles).astype(BF16), jnp.sin(angles).astype(BF16)


def block_tables(length):
    cosine, sine = tables(length)
    left = jnp.concatenate(
        [jnp.concatenate([cosine, sine], 1), jnp.concatenate([-sine, cosine], 1)], 0
    )
    right = jnp.concatenate(
        [jnp.concatenate([cosine, -sine], 1), jnp.concatenate([sine, cosine], 1)], 0
    )
    return left, right


def dot(left_side, right_side):
    return jnp.dot(left_side, right_side, preferred_element_type=F32)


def cost(flops, moved):
    return pl.CostEstimate(flops=int(flops), bytes_accessed=int(moved), transcendentals=0)


def spec(shape, index=None):
    rank = len(shape)
    return pl.BlockSpec(shape, index or (lambda *_: (0,) * rank))


SCALARS = pl.BlockSpec(memory_space=pltpu.SMEM)
WHOLE = pl.BlockSpec(memory_space=pltpu.VMEM)
UNROLL = 8
STEP = 8
LANES = 128


def column_row(cols_ref, owner, count):
    return cols_ref[:, pl.ds(pl.multiple_of(owner * count, LANES), count)]


def flip(cols, ny, nz):
    return lax.rem(ny - cols // nz, ny) * nz + lax.rem(nz - cols % nz, nz)


def one_hot(row, base, size):
    position = lax.broadcasted_iota(jnp.int32, (size, row.shape[1]), 0) + base
    return jnp.where(row == position, 1.0, 0.0).astype(BF16)


def dot_t(left_side, right_side):
    dims = (((1,), (1,)), ((), ()))
    return lax.dot_general(left_side, right_side, dims, preferred_element_type=F32)


def mirror_kernel(span, nz, me_ref, kernel_ref, cols_ref, out_ref, first_ref):
    nx, count = kernel_ref.shape
    row = lax.broadcasted_iota(jnp.int32, (nx, nx), 0)
    column = lax.broadcasted_iota(jnp.int32, (nx, nx), 1)
    swap = jnp.where(lax.rem(row + column, nx) == 0, 1.0, 0.0).astype(BF16)
    mirrored = dot(swap, kernel_ref[...].astype(BF16)).astype(BF16)
    out_ref[...] = mirrored
    local_cols = column_row(cols_ref, me_ref[0], count) - me_ref[0] * span
    target = jnp.where(local_cols < nz, lax.rem(nz - local_cols, nz), -1)
    first_ref[...] = dot_t(mirrored, one_hot(target, 0, nz)).astype(BF16)


def mirror(me, kernel, cols, span, nz):
    nx = kernel.shape[0]
    return pl.pallas_call(
        functools.partial(mirror_kernel, span, nz),
        out_shape=[jax.ShapeDtypeStruct(kernel.shape, BF16), jax.ShapeDtypeStruct((nx, nz), BF16)],
        in_specs=[SCALARS, WHOLE, WHOLE],
        out_specs=[WHOLE] * 2,
        cost_estimate=cost(2 * nx * nx * kernel.shape[1], 6 * kernel.size),
        name="mirror",
    )(me, kernel, cols)


def expand_kernel(scale, groups, span, ny, me_ref, own_ref, neg_ref, first_ref, cols_ref, out_ref, hot):
    nx, count = own_ref.shape
    length = out_ref.shape[2]
    wide = 2 * length
    me = me_ref[0]
    both = jnp.concatenate([own_ref[...].astype(BF16), neg_ref[...]], 1)
    mine = column_row(cols_ref, me, count) - me * span
    theirs = flip(column_row(cols_ref, groups - 1 - me, count), ny, length) - me * span
    group = jnp.concatenate([mine, theirs + span], 1) // wide
    group = group - jnp.concatenate(
        [jnp.zeros((1, count), jnp.int32), jnp.full((1, count), span // wide, jnp.int32)], 1
    )
    hot[:, :count] = one_hot(mine & (wide - 1), 0, wide)
    hot[:, count:] = one_hot(theirs & (wide - 1), 0, wide)

    def step(number, carry):
        sides = []
        for k in range(2):
            wanted = jnp.where(group == 2 * number + k, 1.0, 0.0).astype(BF16)
            sides.append(both * wanted)
        total = dot_t(jnp.concatenate(sides, 0), hot[...])
        for k in range(2):
            for half in range(2):
                out_ref[4 * number + 2 * k + half] = (
                    total[k * nx : (k + 1) * nx, half * length : (half + 1) * length] * scale
                )
        return carry

    lax.fori_loop(0, out_ref.shape[0] // 4, step, 0)
    out_ref[0] = out_ref[0] + first_ref[...].astype(F32) * scale


def expand(me, kernel, neg, first, cols, groups, ny, length, scale):
    nx, count = kernel.shape
    rows = ny // groups
    return pl.pallas_call(
        functools.partial(expand_kernel, scale, groups, rows * length, ny),
        out_shape=jax.ShapeDtypeStruct((rows, nx, length), F32),
        in_specs=[SCALARS] + [WHOLE] * 4,
        out_specs=WHOLE,
        scratch_shapes=[pltpu.VMEM((2 * length, 2 * count), BF16)],
        cost_estimate=cost(4 * nx * count * rows * length, 4 * nx * (count + rows * length)),
        name="expand",
    )(me, kernel, neg, first, cols)


PAD = 1


def unload(hold, first, out_ref):
    lines, _, count, _ = out_ref.shape

    def step(line, carry):
        for c in range(2):
            out_ref[line, c] = hold[c, pl.ds((first + line) * (count + PAD), count), :].astype(BF16)
        return carry

    lax.fori_loop(0, lines, step, 0, unroll=min(8, lines))


def forward_kernel(parts, base, cuts, me_ref, grid_ref, own_ref, *refs):
    piece_refs = refs[:parts]
    if parts > 1:
        zt_ref, yt_ref, their_ref = refs[parts : parts + 3]
        per = piece_refs[0].shape[0]
        for slot, piece_ref in enumerate(piece_refs):
            their_ref[pl.ds((me_ref[0] ^ slot) * per, per)] = piece_ref[...]
    else:
        their_ref, zt_ref, yt_ref = refs[:3]
    out_refs, hold = refs[3 + parts - (parts == 1) : -1], refs[-1]
    count, ny, nz = own_ref.shape[1:]
    tiles = ny // their_ref.shape[1]
    zt, yt = zt_ref[...], yt_ref[...]

    def step(pair, carry):
        lines = []
        for k in range(2):
            x = 2 * pair + k
            theirs = their_ref[pl.ds((base + x) * tiles, tiles)].reshape(ny, nz)
            lines.append(jnp.concatenate([own_ref[0, x] * theirs, own_ref[1, x] * theirs], 1))
        first = dot(jnp.concatenate(lines, 0), zt).astype(BF16)
        stack = jnp.concatenate(
            [
                jnp.concatenate([first[:ny, :nz], first[ny:, :nz]], 1),
                jnp.concatenate([first[:ny, nz:], first[ny:, nz:]], 1),
            ],
            0,
        )
        second = dot(yt, stack)
        for k in range(2):
            for c in range(2):
                hold[c, pl.ds(2 * pair + k, ny, stride=count + PAD), :] = second[
                    c * ny : (c + 1) * ny, k * nz : (k + 1) * nz
                ]
        return carry

    lax.fori_loop(0, count // 2, step, 0, unroll=min(UNROLL, count // 2))
    part = ny // len(out_refs)
    for number, out_ref in enumerate(out_refs):
        owner = grid_ref[0] ^ (number // cuts)
        unload(hold, (owner * cuts + number % cuts) * part, out_ref)


def forward(me, grid_pos, own, pieces, half, count, zt, yt, groups, cuts):
    ny, nz = own.shape[2:]
    part = ny // (groups * cuts)
    parts = len(pieces)
    shape = jax.ShapeDtypeStruct((part, 2, count, nz), BF16)
    their = jax.ShapeDtypeStruct((parts * pieces[0].shape[0],) + pieces[0].shape[1:], BF16)
    outs = ([their] if parts > 1 else []) + [shape] * (groups * cuts)
    return pl.pallas_call(
        functools.partial(forward_kernel, parts, half * count, cuts),
        grid=(1,),
        out_shape=outs,
        in_specs=[SCALARS, SCALARS, spec((2, count, ny, nz), lambda i: (0, half, 0, 0))]
        + [spec(p.shape) for p in pieces]
        + [spec(zt.shape), spec(yt.shape)],
        out_specs=[spec(o.shape) for o in outs],
        scratch_shapes=[pltpu.VMEM((2, ny * (count + PAD), nz), F32)],
        cost_estimate=cost(2 * count * ny * nz * 2 * (2 * ny + 2 * nz), 12 * count * ny * nz),
        name="forward",
    )(me, grid_pos, own, *pieces, zt, yt)


def middle_kernel(groups, halves, grid_ref, *refs):
    in_refs = refs[:groups]
    kern_ref, xt_ref, ixt_ref = refs[groups : groups + 3]
    out_refs, hold = refs[groups + 3 : -1], refs[-1]
    count, nx, nz = kern_ref.shape
    xt, ixt = xt_ref[...], ixt_ref[...]

    def step(pair, carry):
        lines, factors = [], []
        for k in range(2):
            line = 2 * pair + k
            lines.append(jnp.concatenate([r[line, c] for c in range(2) for r in in_refs], 0))
            factors.append(kern_ref[line])
        factor = jnp.concatenate(factors, 1)
        spectrum = dot(xt, jnp.concatenate(lines, 1))
        scaled = jnp.concatenate(
            [(spectrum[:nx] * factor).astype(BF16), (spectrum[nx:] * factor).astype(BF16)], 0
        )
        third = dot(ixt, scaled)
        for k in range(2):
            for c in range(2):
                hold[c, pl.ds(2 * pair + k, nx, stride=count + PAD), :] = third[
                    c * nx : (c + 1) * nx, k * nz : (k + 1) * nz
                ]
        return carry

    lax.fori_loop(0, count // 2, step, 0, unroll=min(UNROLL, count // 2))
    rows = nx // (groups * halves)
    for number, out_ref in enumerate(out_refs):
        owner = grid_ref[0] ^ (number // halves)
        unload(hold, (owner * halves + number % halves) * rows, out_ref)


def middle(grid_pos, pieces, kern, cut, xt, ixt, halves):
    groups = len(pieces)
    count, nx, nz = pieces[0].shape[0], kern.shape[1], kern.shape[2]
    rows = nx // (groups * halves)
    shape = jax.ShapeDtypeStruct((rows, 2, count, nz), BF16)
    return pl.pallas_call(
        functools.partial(middle_kernel, groups, halves),
        grid=(1,),
        out_shape=[shape] * (groups * halves),
        in_specs=[SCALARS]
        + [spec(p.shape) for p in pieces]
        + [spec((count, nx, nz), lambda i: (cut, 0, 0)), spec(xt.shape), spec(ixt.shape)],
        out_specs=[spec(shape.shape)] * (groups * halves),
        scratch_shapes=[pltpu.VMEM((2, nx * (count + PAD), nz), F32)],
        cost_estimate=cost(16 * nx * nx * count * nz, 12 * count * nx * nz),
        name="middle",
    )(grid_pos, *pieces, kern, xt, ixt)


def backward_kernel(number, has_total, *refs):
    in_refs = refs[:number]
    their_ref, weight_ref, yt_ref, zt_ref = refs[number : number + 4]
    total_ref = refs[number + 4] if has_total == 2 else None
    out_ref = refs[-1]
    count, ny, nz = out_ref.shape[1:]
    tiles = ny // their_ref.shape[1]
    zt, yt = zt_ref[...], yt_ref[...]
    weight = weight_ref[0]

    def step(pair, carry):
        lines = []
        for k in range(2):
            x = 2 * pair + k
            lines.append(jnp.concatenate([r[x, c] for c in range(2) for r in in_refs], 0))
        fourth = dot(yt, jnp.concatenate(lines, 1)).astype(BF16)
        stack = jnp.concatenate(
            [
                jnp.concatenate([fourth[:ny, k * nz : (k + 1) * nz], fourth[ny:, k * nz : (k + 1) * nz]], 1)
                for k in range(2)
            ],
            0,
        )
        potential = dot(stack, zt)
        for k in range(2):
            x = 2 * pair + k
            theirs = their_ref[pl.ds(x * tiles, tiles)].reshape(ny, nz).astype(F32) * weight
            for n in range(2):
                term = potential[k * ny : (k + 1) * ny, n * nz : (n + 1) * nz] * theirs
                if total_ref is None:
                    out_ref[n, x] = -term
                else:
                    out_ref[n, x] = total_ref[n, x] - term
        return carry

    lax.fori_loop(0, count // 2, step, 0, unroll=min(UNROLL, count // 2))


def backward(pieces, bases, their, weight, yt, zt, total, accumulate, part_number, count, slab):
    ny, nz = sum(p.shape[2] for p in pieces), pieces[0].shape[3]
    number = len(pieces)
    step = min(STEP, count)
    steps = count // step
    begin = part_number * steps
    tiles = ny // their.shape[1]
    block = spec((2, step, ny, nz), lambda i: (0, begin + i, 0, 0))
    has_total = 0 if total is None else (2 if accumulate else 1)
    extra = [] if total is None else [total]
    extra_specs = [] if total is None else [block if accumulate else pl.BlockSpec(memory_space=pl.ANY)]

    def rows_of(piece, base):
        return spec((step,) + piece.shape[1:], lambda i: (base // step + i, 0, 0, 0))

    return pl.pallas_call(
        functools.partial(backward_kernel, number, has_total),
        grid=(steps,),
        out_shape=jax.ShapeDtypeStruct((2, slab, ny, nz), F32),
        in_specs=[rows_of(p, b) for p, b in zip(pieces, bases)]
        + [spec((step * tiles,) + their.shape[1:], lambda i: (begin + i, 0, 0))]
        + [SCALARS, spec(yt.shape), spec(zt.shape)]
        + extra_specs,
        out_specs=block,
        input_output_aliases={number + 4: 0} if extra else {},
        cost_estimate=cost(2 * count * ny * nz * 2 * (2 * ny + 2 * nz), 24 * count * ny * nz),
        name="backward",
    )(*pieces, their, weight, yt, zt, *extra)


TILE = 16


def after(value, *others):
    return lax.optimization_barrier((value, others))[0]


def shift(value, axis, size, mask):
    return lax.ppermute(value, axis, [(i, i ^ mask) for i in range(size)]) if mask else value


def split_kernel(me_ref, in_ref, *out_refs):
    per = out_refs[0].shape[0]
    for slot, out_ref in enumerate(out_refs):
        out_ref[...] = in_ref[0, pl.ds((me_ref[0] ^ slot) * per, per)]


def split(me, value, band, chunk, tiles, parts):
    shape = jax.ShapeDtypeStruct((tiles // parts,) + value.shape[2:], value.dtype)
    return pl.pallas_call(
        split_kernel,
        grid=(1,),
        out_shape=[shape] * parts,
        in_specs=[SCALARS, spec((1, tiles) + value.shape[2:], lambda i: (band, chunk, 0, 0))],
        out_specs=[spec(shape.shape)] * parts,
        cost_estimate=cost(0, 4 * tiles * TILE * value.shape[3]),
        name="split",
    )(me, value)


def pick_kernel(parts, choice_ref, *refs):
    in_refs, out_refs, hold = refs[:parts], refs[parts:-1], refs[-1]
    for slot, in_ref in enumerate(in_refs):
        hold[slot] = in_ref[...]
    for slot, out_ref in enumerate(out_refs):
        out_ref[...] = hold[choice_ref[slot]]


def pick(choice, pieces):
    parts, shape = len(pieces), pieces[0].shape
    return pl.pallas_call(
        functools.partial(pick_kernel, parts),
        out_shape=[jax.ShapeDtypeStruct(shape, pieces[0].dtype)] * parts,
        in_specs=[SCALARS] + [WHOLE] * parts,
        out_specs=[WHOLE] * parts,
        scratch_shapes=[pltpu.VMEM((parts,) + shape, pieces[0].dtype)],
        cost_estimate=cost(0, 4 * parts * math.prod(shape)),
        name="pick",
    )(choice, *pieces)


def local(orbitals, occupation, partner, col_index, kernel):
    bands, groups = lax.axis_size("band"), lax.axis_size("grid")
    slab, ny, nz = orbitals.shape[1:]
    nx, _ = kernel.shape
    lines = ny // groups
    band_pos, me = lax.axis_index("band"), lax.axis_index("grid")
    band_slots = jnp.arange(bands, dtype=jnp.int32)
    my_band = band_pos.astype(jnp.int32).reshape(1)
    choice = jnp.take(partner, band_slots ^ band_pos) ^ band_pos
    tiled = orbitals.reshape(2, slab * ny // TILE, TILE, nz)

    def swap(value, slot):
        return shift(value, "grid", groups, slot)

    def slotwise(sent, near_after=None):
        moved = []
        for slot, piece in enumerate(sent):
            if near_after is not None and slot < bands // 2:
                piece = after(piece, near_after)
            moved.append(shift(piece, "band", bands, slot))
        return moved

    my_grid = me.astype(jnp.int32).reshape(1)
    cols = col_index.reshape(1, -1)
    blocks = tiled[0].reshape(bands, -1, TILE, nz)
    sent = [
        lax.dynamic_index_in_dim(blocks, band_pos ^ slot, 0, keepdims=False) for slot in range(bands)
    ]
    arrived = slotwise(sent)
    sent1 = split(my_band, after(tiled, *sent), 1, 0, slab * ny // TILE, bands)

    mirror_of = [(i, groups - 1 - i) for i in range(groups)]
    mirror_first = [(i, (groups - i) % groups) for i in range(groups)]
    mirrored, first_line = mirror(my_grid, after(kernel, *sent), cols, lines * nz, nz)
    neg = lax.ppermute(mirrored, "grid", mirror_of)
    first = lax.ppermute(first_line, "grid", mirror_first)

    def slots(table, axis):
        shape = table.shape
        blocks = table.reshape(shape[:axis] + (2, groups, shape[axis] // (2 * groups)) + shape[axis + 1 :])
        order = jnp.arange(groups, dtype=jnp.int32) ^ me
        return jnp.take(blocks, order, axis=axis + 1).reshape(shape)

    xleft, xright = block_tables(nx)
    yleft, yright = block_tables(ny)
    zleft, zright = block_tables(nz)
    x_forward, y_inverse = slots(xleft, 1), slots(yright, 1)
    cuts = 2 if lines % 32 == 0 else 1
    parts = 2 if slab % 32 == 0 else 1

    picked = pick(choice, after(arrived, mirrored, first_line, *sent1))
    fetched = slotwise(picked)
    kern = expand(
        my_grid, after(kernel, *picked), neg, first, cols, groups, ny, nz, 0.5 / (nx * ny * nz)
    )
    arrived = slotwise(after(sent1, kern))

    def outward(pieces):
        outs = forward(my_band, my_grid, orbitals, pieces, 0, slab, zright, yleft, groups, cuts)
        their, sent = (outs[0], outs[1:]) if len(pieces) > 1 else (pieces[0], outs)
        moved = [
            [swap(sent[slot * cuts + cut], slot) for slot in range(groups)]
            for cut in range(cuts)
        ]
        return their, sent, moved

    their0, sent, moved0 = outward(fetched)
    picked = pick(choice, after(arrived, *sent))

    def centre(cut, moved, halves):
        return middle(my_grid, moved[cut], kern, cut, x_forward, xright, halves)

    def home(values):
        return [swap(value, slot) for slot, value in enumerate(values)]

    def ending(m, total, back, bases, h, count, their):
        weight = lax.dynamic_slice_in_dim(occupation, partner[band_pos] * 2 + m, 1, 0)
        pieces = [piece for by_cut in zip(*back) for piece in by_cut]
        return backward(
            pieces, bases * groups, their, weight, y_inverse, zleft, total, m > 0, h, count, slab
        )

    answers = [centre(cut, moved0, 1) for cut in range(cuts)]
    back0 = [home(answers[cut]) for cut in range(cuts)]
    fetched = slotwise(picked, near_after=answers[0])
    their1, _, moved1 = outward(after(fetched, *answers[-1]))

    last = cuts - 1
    answers = [centre(cut, moved1, parts if cut == last else 1) for cut in range(cuts)]
    early = [home(answers[cut]) for cut in range(last)]
    rows = slab // parts
    late = [answers[last][h::parts] for h in range(parts)]
    late[0] = home(late[0])
    total = None
    for h in range(parts):
        if h == parts - 1:
            back0[0] = after(back0[0], *answers[last])
        total = ending(0, total, back0, (h * rows,) * cuts, h, rows, their0)
    for h in range(1, parts):
        late[h] = home(after(late[h], total))
    for h in range(parts):
        bases = (h * rows,) * last + (0,)
        total = ending(1, total, early + [late[h]], bases, h, rows, their1)
    return total


def solution(mesh):
    in_specs = (P("band", "grid", None, None), P(), P(), P(), P(None, "grid"))
    out_specs = P("band", "grid", None, None)
    return jax.shard_map(local, mesh=mesh, in_specs=in_specs, out_specs=out_specs, check_vma=False)
```
